32 devices in a mesh: grp: 2 (over y), row: 4 (over x, core), slab: 4 (over z).
Axes of the slice: x: 2, y: 2, z: 4, core: 2. Of those that a mesh axis runs over, the one named last changes fastest.
Arguments:
- observed: float32 [128, 256, 256], P(('grp', 'slab'), 'row'), parts along dimension 0, may hold values from 0.25 to 4
- band_index: int32 [64], P('slab'), may hold values from 0 to 15
- taps_x: float32 [16, 31], replicated, may hold values from 0.005 to 0.12
- taps_y: float32 [16, 31], replicated, may hold values from 0.005 to 0.12
- taps_z: float32 [31], replicated, may hold values from 0.005 to 0.12
Outputs:
- estimate: float32 [128, 256, 256], P(('grp', 'slab'), 'row'), parts along dimension 0
The draws below stay inside these ranges and needn't reach their ends.
There are 2 independent parts, one for each index of `grp`. The reference program is written for one: setup_inputs(seed, part) draws one part's arguments, and reference() takes and returns one part's arrays. A program takes and returns all parts, laid end to end along the dimension named above; an argument that names none is the same for every part. Nothing has to cross between parts.
All inputs are finite; a program needn't handle non-finite values.
Results may differ from the reference program's by a relative error of at most 0.00015.
Values sent between devices are 32-bit elements; how exact they have to be, the bound alone decides.
A program may use at most 64 MiB of HBM per device.

```python
import math
import jax
import jax.numpy as jnp
from jax import lax

NY = 256
TAPS = 31
NB = 16
ITERS = 2
NX = 256
NZ = 64


def plant(array, key, least, top_value):
    extent = array.shape
    place = [jax.random.randint(jax.random.fold_in(key, axis), (), 0, extent[axis]) for axis in range(len(extent))]
    array = array.at[tuple(place)].set(least)
    longest = extent.index(max(extent))
    place[longest] = (place[longest] + 1) % extent[longest]
    return array.at[tuple(place)].set(top_value)


def block_scale(own_key, extent, pieces, low, top_value):
    gain = 1.0
    for position, parts in pieces:
        heights = jax.random.uniform(jax.random.fold_in(jax.random.fold_in(own_key, 6), position), (parts,), jnp.float32, low / len(pieces), top_value / len(pieces))
        gain = gain * jnp.repeat(jnp.exp(heights), extent[position] // parts).reshape((-1,) + (1,) * (len(extent) - 1 - position))
    return gain


def setup_inputs(seed: int = 0, part: int = 0) -> dict:
    keys = jax.random.split(jax.random.key(seed), 6)
    own_keys = jax.random.split(jax.random.fold_in(keys[5], part), 6)
    return {
        "observed": jnp.clip(0.25 + 3.75 * jax.random.uniform(own_keys[0], (NZ, NX, NY), jnp.float32) ** block_scale(own_keys[0], (NZ, NX, NY), ((0, 4), (1, 4)), -0.2, 0.2), 0.25, 4.0),
        "band_index": plant(jax.random.randint(keys[1], (NZ,), 0, NB), jax.random.fold_in(keys[1], 1), 0, NB - 1).astype(jnp.int32),
        "taps_x": jnp.clip(jnp.exp(jax.random.uniform(keys[2], (NB, TAPS), jnp.float32, math.log(0.005), math.log(0.12))), 0.005, 0.12),
        "taps_y": jnp.clip(jnp.exp(jax.random.uniform(keys[3], (NB, TAPS), jnp.float32, math.log(0.005), math.log(0.12))), 0.005, 0.12),
        "taps_z": jnp.clip(jnp.exp(jax.random.uniform(keys[4], (TAPS,), jnp.float32, math.log(0.005), math.log(0.12))), 0.005, 0.12),
    }


def correlate(field, taps, dim):
    radius = taps.shape[-1] // 2
    length = field.shape[dim]
    widths = [(0, 0), (0, 0), (0, 0)]
    widths[dim] = (radius, radius)
    padded = jnp.pad(field, widths)
    total = jnp.zeros(field.shape, jnp.float32)
    for k in range(taps.shape[-1]):
        piece = lax.slice_in_dim(padded, k, k + length, axis=dim)
        if taps.ndim == 2:
            weight = taps[:, k][:, None, None]
        else:
            weight = taps[k]
        total = total + weight * piece
    return total


def forward(field, plane_x, plane_y, taps_z):
    field = correlate(field, plane_x, 1)
    field = correlate(field, plane_y, 2)
    return correlate(field, taps_z, 0)


def adjoint(field, plane_x, plane_y, taps_z):
    field = correlate(field, taps_z[::-1], 0)
    field = correlate(field, plane_y[:, ::-1], 2)
    return correlate(field, plane_x[:, ::-1], 1)


def reference(observed, band_index, taps_x, taps_y, taps_z):
    plane_x = taps_x[band_index]
    plane_y = taps_y[band_index]
    norm = adjoint(jnp.ones(observed.shape, jnp.float32), plane_x, plane_y, taps_z)
    estimate = observed
    for step in range(ITERS):
        blurred = forward(estimate, plane_x, plane_y, taps_z)
        ratio = observed / blurred
        estimate = estimate * adjoint(ratio, plane_x, plane_y, taps_z) / norm
    return estimate
```

```python
import functools

import jax
import jax.numpy as jnp
from jax import lax
from jax.experimental import pallas as pl
from jax.experimental.pallas import tpu as pltpu
from jax.sharding import PartitionSpec as P

ITERS = 2
CHUNK = 16
LANES = 128
UNROLL = 8
F32 = jnp.float32
BF16 = jnp.bfloat16


def split(v):
    high = v.astype(BF16)
    return high, (v - high.astype(F32)).astype(BF16)


def chunk_order(count, it):
    first = [1, 0] if it == 0 else [0, 1]
    inner = list(range(2, count - 1))
    return first + ([count - 1] + inner if it == ITERS - 1 else inner + [count - 1])


def kernel(
    rows_n, slabs_n, taps,
    band_hbm, tz_hbm, tx_hbm, ty_hbm, obs_hbm,
    out_ref,
    band_ref, tz_ref, tx_ref, ty_ref, in_sem,
    txf_ref, txr_ref, tyf_ref, tyr_ref, ext, dext, bz, rz, wf_h, wf_l, wa_h, wa_l, af, aa,
    zs_sem, zr_sem, xs_sem, xr_sem,
):
    depth, height, width = obs_hbm.shape
    radius = taps // 2
    halo = CHUNK
    chunks = height // CHUNK
    row = lax.axis_index("row")
    slab = lax.axis_index("slab")
    parity = row % 2

    def chunk(p):
        return p + parity * (chunks - 1 - 2 * p)

    def begin(p, more=0, unit=CHUNK):
        return pl.multiple_of(chunk(p) * CHUNK + more, unit)

    fetches = [
        pltpu.make_async_copy(src, dst, in_sem.at[n])
        for n, (src, dst) in enumerate((
            (obs_hbm, ext.at[0, :, pl.ds(halo, height), :]),
            (ty_hbm, ty_ref), (tx_hbm, tx_ref), (band_hbm, band_ref), (tz_hbm, tz_ref),
        ))
    ]
    for fetch in fetches:
        fetch.start()

    sides = {
        ("row", 0): (row < rows_n - 1, row + 1),
        ("row", 1): (row > 0, row - 1),
        ("slab", 0): (slab < slabs_n - 1, slab + 1),
        ("slab", 1): (slab > 0, slab - 1),
    }

    barrier = pltpu.get_barrier_semaphore()
    for (axis, _), (there, index) in sides.items():
        @pl.when(there)
        def _(axis=axis, index=index):
            pl.semaphore_signal(barrier, inc=1, device_id={axis: index}, device_id_type=pl.DeviceIdType.MESH)

    def clear(axis, buffer, it):
        for side in range(2):
            @pl.when(jnp.logical_not(sides[(axis, side)][0]))
            def _():
                if axis == "row":
                    first = 0 if side == 1 else halo + height
                    buffer[it, :, first:first + halo, :] = jnp.zeros((depth, halo, width), F32)
                else:
                    first = 0 if side == 1 else radius + depth
                    buffer[it, first:first + radius] = jnp.zeros((radius, height, width), F32)

    pl.semaphore_wait(barrier, sum(there.astype(jnp.int32) for there, _ in sides.values()))

    def row_copy(src, dst, it, which, side):
        if side == 0:
            src_start, dst_start = src[1] + height - halo, 0
        else:
            src_start, dst_start = src[1], halo + height
        return pltpu.make_async_remote_copy(
            src_ref=src[0].at[:, pl.ds(src_start, halo), :],
            dst_ref=dst.at[it, :, pl.ds(dst_start, halo), :],
            send_sem=xs_sem.at[it, which, side],
            recv_sem=xr_sem.at[it, which, side],
            device_id={"row": sides[("row", side)][1]},
            device_id_type=pl.DeviceIdType.MESH,
        )

    def slab_copy(buf, it, which, c, side):
        if side == 0:
            src_start, dst_start = depth, 0
        else:
            src_start, dst_start = radius, radius + depth
        span = pl.ds(begin(c), CHUNK)
        return pltpu.make_async_remote_copy(
            src_ref=buf.at[it, pl.ds(src_start, radius), span, :],
            dst_ref=buf.at[it, pl.ds(dst_start, radius), span, :],
            send_sem=zs_sem.at[it, which, c, side],
            recv_sem=zr_sem.at[it, which, c, side],
            device_id={"slab": sides[("slab", side)][1]},
            device_id_type=pl.DeviceIdType.MESH,
        )

    def start(axis, side, make, also=True):
        @pl.when(sides[(axis, side)][0] & also)
        def _():
            make(side).start()

    def recv(axis, side, make, also=True):
        @pl.when(sides[(axis, 1 - side)][0] & also)
        def _():
            make(side).wait_recv()

    def sent(axis, side, make):
        @pl.when(sides[(axis, side)][0])
        def _():
            make(side).wait_send()

    sends = []

    def x_make(it, which):
        buffer = ext if which == 0 else dext
        return functools.partial(row_copy, (buffer.at[it], halo), buffer, it, which)

    def z_make(it, which, c):
        return functools.partial(slab_copy, bz if which == 0 else rz, it, which, c)

    def x_start(it, which, p):
        near = p == 0
        for v in range(2):
            side = 1 - v if near else v
            start("row", side, x_make(it, which), parity == v)
        if near:
            sends.extend(("row", side, x_make(it, which)) for side in range(2))

    def x_recv(it, which, p):
        near = p == 0
        for v in range(2):
            recv("row", v if near else 1 - v, x_make(it, which), parity == v)

    def z_start(it, which, c):
        for side in range(2):
            start("slab", side, z_make(it, which, c))
            sends.append(("slab", side, z_make(it, which, c)))

    def z_recv(it, which, c):
        for side in range(2):
            recv("slab", side, z_make(it, which, c))

    fetches[0].wait()
    for p in (0, chunks - 1):
        x_start(0, 0, p)
    for fetch in fetches[1:]:
        fetch.wait()

    kk = 3 * halo
    mirror = (
        lax.broadcasted_iota(jnp.int32, (LANES, LANES), 0) + lax.broadcasted_iota(jnp.int32, (LANES, LANES), 1)
        == taps - 1
    ).astype(F32)
    for source, ahead, back in ((tx_ref, txf_ref, txr_ref), (ty_ref, tyf_ref, tyr_ref)):
        ahead[...] = jnp.zeros(ahead.shape, F32)
        ahead[:, 0:taps] = source[...]
        back[...] = jnp.dot(ahead[...], mirror, precision=lax.Precision.HIGHEST, preferred_element_type=F32)

    gap = lax.broadcasted_iota(jnp.int32, (LANES, LANES), 0) - lax.broadcasted_iota(jnp.int32, (LANES, LANES), 1)
    blocks = range(width // LANES)

    def column_band(line):
        ring = pltpu.roll(jnp.broadcast_to(line, (LANES, LANES)), LANES - radius, 1, stride=1, stride_axis=0)

        def block(offset):
            near = gap + offset * LANES
            return jnp.where((near <= radius) & (near >= -radius), ring, 0.0)
        made = {offset: block(offset) for offset in (-1, 0, 1)}
        return [[made.get(i - j) for j in blocks] for i in blocks]

    def store_band(w_h, w_l, z, band, scale):
        for i in blocks:
            for j in blocks:
                part = jnp.zeros((LANES, LANES), F32) if band[i][j] is None else band[i][j]
                if scale is not None:
                    part = part * scale[j]
                high, low = split(part)
                w_h[z, i * LANES:(i + 1) * LANES, j * LANES:(j + 1) * LANES] = high
                w_l[z, i * LANES:(i + 1) * LANES, j * LANES:(j + 1) * LANES] = low

    def store_rows(a):
        high = a.astype(BF16).astype(F32)
        low = a - high
        zero = jnp.zeros(a.shape, F32)
        first = jnp.concatenate([high, zero], axis=1)
        second = jnp.concatenate([low, zero], axis=1)
        return (first + pltpu.roll(second, kk, 1) + pltpu.roll(first, 2 * kk, 1)).astype(BF16)

    def row_band(line):
        return pltpu.roll(jnp.broadcast_to(line, (CHUNK, LANES)), halo - radius, 1, stride=1, stride_axis=0)

    def build_forward(z, carry):
        at = pl.ds(band_ref[z], 1)
        store_band(wf_h, wf_l, z, column_band(tyr_ref[at, :]), None)
        af[z] = store_rows(row_band(txf_ref[at, :]))
        return carry

    def build_adjoint(z, carry):
        at = pl.ds(band_ref[z], 1)
        band = column_band(tyf_ref[at, :])
        lane = lax.broadcasted_iota(jnp.int32, (1, LANES), 1)
        tzv = jnp.zeros((1, LANES), F32)
        for k in range(taps):
            tzv = jnp.where(lane == k, tz_ref[k], tzv)
        plane = slab * depth + z + radius - lane
        inside = (plane >= 0) & (plane < slabs_n * depth)
        cz = jnp.sum(jnp.where(inside, tzv, 0.0), axis=1, keepdims=True)
        scale = []
        for j in blocks:
            total = sum(jnp.sum(band[i][j], axis=0, keepdims=True) for i in blocks if band[i][j] is not None)
            scale.append(1.0 / (total * cz))
        store_band(wa_h, wa_l, z, band, scale)
        base = row_band(txr_ref[at, :])
        for c in range(chunks):
            at_row = row * height + (c - 1) * CHUNK + lax.broadcasted_iota(jnp.int32, (CHUNK, LANES), 1)
            inside = (at_row >= 0) & (at_row < rows_n * height)
            aa[z, c] = store_rows(base / jnp.sum(jnp.where(inside, base, 0.0), axis=1, keepdims=True))
        return carry

    def blur_rows(a, v):
        high, low = split(v)
        return jnp.dot(a[:, :3 * kk], jnp.concatenate([high, high, low], axis=0), preferred_element_type=F32)

    def blur_columns(v, w_h, w_l):
        high, low = split(v)
        n = v.shape[0]
        both = jnp.dot(jnp.concatenate([high, low], axis=0), w_h, preferred_element_type=F32)
        return both[:n] + both[n:] + jnp.dot(high, w_l, preferred_element_type=F32)

    def edge(it, which, p):
        if p in (0, chunks - 1):
            x_recv(it, which, p)

    def stage_xy(it, p):
        edge(it, 0, p)
        c = begin(p)

        def body(z, carry):
            v = blur_rows(af[z], ext[it, z, pl.ds(c, kk), :])
            bz[it, radius + z, pl.ds(c, CHUNK), :] = blur_columns(v, wf_h[z], wf_l[z])
            return carry
        lax.fori_loop(0, depth, body, 0, unroll=8)
        z_start(it, 0, p)

    def blur_depth(buf, it, tile, lanes, flip):
        total = None
        for k in range(taps):
            weight = tz_ref[taps - 1 - k] if flip else tz_ref[k]
            term = weight * buf[it, k:k + depth, tile, lanes]
            total = term if total is None else total + term
        return total

    def tiles(p):
        for r in range(0, CHUNK, 8):
            for l in range(0, width, LANES):
                yield pl.ds(begin(p, r, 8), 8), pl.ds(begin(p, halo + r, 8), 8), slice(l, l + LANES)

    def stage_ratio(it, p):
        for tile, inner, lanes in tiles(p):
            blurred = blur_depth(bz, it, tile, lanes, False)
            rz[it, radius:radius + depth, tile, lanes] = ext[0, :, inner, lanes] / blurred
        z_start(it, 1, p)

    def stage_zy(it, p):
        for tile, inner, lanes in tiles(p):
            dext[it, :, inner, lanes] = blur_depth(rz, it, tile, lanes, True)
        rows = pl.ds(begin(p, halo), CHUNK)

        def body(z, carry):
            dext[it, z, rows, :] = blur_columns(dext[it, z, rows, :], wa_h[z], wa_l[z])
            return carry
        lax.fori_loop(0, depth, body, 0, unroll=8)
        if p in (0, chunks - 1):
            x_start(it, 1, p)

    def stage_x(it, p):
        edge(it, 1, p)
        c = begin(p)
        inner = pl.ds(begin(p, halo), CHUNK)

        def body(z, carry):
            v = ext[it, z, inner, :] * blur_rows(aa[z, chunk(p)], dext[it, z, pl.ds(c, kk), :])
            if it == ITERS - 1:
                out_ref[z, pl.ds(c, CHUNK), :] = v
            else:
                ext[it + 1, z, inner, :] = v
            return carry
        lax.fori_loop(0, depth, body, 0, unroll=8)
        if it < ITERS - 1 and p in (0, chunks - 1):
            x_start(it + 1, 0, p)

    clear("row", ext, 0)
    lax.fori_loop(0, depth, build_forward, 0, unroll=2)
    started = 0
    for it in range(ITERS):
        order = chunk_order(chunks, it)
        for p in order[started:]:
            stage_xy(it, p)
        if it == 0:
            lax.fori_loop(0, depth, build_adjoint, 0)
            for buffer in (bz, rz):
                for i in range(ITERS):
                    clear("slab", buffer, i)
            for i in range(ITERS):
                clear("row", dext, i)
            for i in range(1, ITERS):
                clear("row", ext, i)
        for p in order:
            z_recv(it, 0, p)
            stage_ratio(it, p)
        for p in order[:-1]:
            z_recv(it, 1, p)
            stage_zy(it, p)
        if it < ITERS - 1:
            for p in range(chunks - 2):
                stage_x(it, p)
            for p in range(chunks - 3):
                stage_xy(it + 1, p)
            z_recv(it, 1, order[-1])
            stage_zy(it, order[-1])
            stage_x(it, chunks - 2)
            stage_xy(it + 1, chunks - 3)
            stage_x(it, chunks - 1)
            started = chunks - 2
        else:
            early = [p for p in range(chunks) if abs(p - order[-1]) > 1]
            for p in early:
                stage_x(it, p)
            z_recv(it, 1, order[-1])
            stage_zy(it, order[-1])
            for p in range(chunks):
                if p not in early:
                    stage_x(it, p)

    for axis, side, make in sends:
        sent(axis, side, make)


def fast_kernel(
    rows_n, slabs_n, taps,
    band_hbm, tz_hbm, tx_hbm, ty_hbm, obs_hbm,
    out_ref,
    band_ref, tz_ref, tx_ref, ty_ref, in_sem,
    txf_ref, txr_ref, tyf_ref, tyr_ref,
    lines, obs, packed, est, final, back,
    ybuf, left_out, right_out, left_in, right_in, edge,
    wf, wa, fh, fl, ah, al, bw, rw, cbuf,
    ls_sem, lr_sem, is_sem, ir_sem, gs_sem, hs_sem, hr_sem, xs_sem, xr_sem, os_sem, or_sem,
):
    depth, height, width = obs_hbm.shape
    radius = taps // 2
    half = depth // 2
    cols = width // slabs_n
    blocks = range(slabs_n)
    rim = CHUNK
    reach = height + 2 * rim
    row = lax.axis_index("row")
    slab = lax.axis_index("slab")
    lower = (slab >= slabs_n // 2).astype(jnp.int32)
    lane = lax.broadcasted_iota(jnp.int32, (1, LANES), 1)
    first_half = lane < cols

    fetches = [
        pltpu.make_async_copy(src, dst, in_sem.at[n])
        for n, (src, dst) in enumerate((
            (obs_hbm, obs), (ty_hbm, ty_ref), (tx_hbm, tx_ref), (band_hbm, band_ref), (tz_hbm, tz_ref),
        ))
    ]
    for fetch in fetches:
        fetch.start()

    barrier = pltpu.get_barrier_semaphore()
    for d in range(1, slabs_n):
        pl.semaphore_signal(
            barrier, inc=1, device_id={"slab": (slab + d) % slabs_n}, device_id_type=pl.DeviceIdType.MESH)
    beside = ((row < rows_n - 1, row + 1), (row > 0, row - 1))
    for there, index in beside:
        @pl.when(there)
        def _(index=index):
            pl.semaphore_signal(barrier, inc=1, device_id={"row": index}, device_id_type=pl.DeviceIdType.MESH)

    def remote(src, dst, send, recv, axis, index):
        return pltpu.make_async_remote_copy(
            src_ref=src, dst_ref=dst, send_sem=send, recv_sem=recv,
            device_id={axis: index}, device_id_type=pl.DeviceIdType.MESH)

    def block(t):
        return pl.ds(half * t, half)

    for fetch in fetches[1:]:
        fetch.wait()
    mirror = (
        lax.broadcasted_iota(jnp.int32, (LANES, LANES), 0) + lax.broadcasted_iota(jnp.int32, (LANES, LANES), 1)
        == taps - 1
    ).astype(F32)
    for source, ahead, turned in ((tx_ref, txf_ref, txr_ref), (ty_ref, tyf_ref, tyr_ref)):
        ahead[...] = jnp.zeros(ahead.shape, F32)
        ahead[:, 0:taps] = source[...]
        turned[...] = jnp.dot(ahead[...], mirror, precision=lax.Precision.HIGHEST, preferred_element_type=F32)
    for z in range(depth):
        at = pl.ds(band_ref[z], 1)
        for n, table in enumerate((txf_ref, txr_ref, tyf_ref, tyr_ref)):
            lines[slab, n, z:z + 1, :] = table[at, :]

    pl.semaphore_wait(barrier, slabs_n - 1 + sum(there.astype(jnp.int32) for there, _ in beside))

    def lines_copy(d, owner):
        return remote(lines.at[owner], lines.at[owner], ls_sem.at[d - 1], lr_sem.at[owner], "slab", (slab + d) % slabs_n)

    for d in range(1, slabs_n):
        lines_copy(d, slab).start()

    def pack(q):
        base = (q * cols // LANES) * LANES
        low = (q * cols) % LANES == 0

        def body(j, carry):
            a = obs[j, :, base:base + LANES]
            b = obs[half + j, :, base:base + LANES]
            if low:
                v = jnp.where(first_half, a, pltpu.roll(b, cols, 1))
            else:
                v = jnp.where(first_half, pltpu.roll(a, cols, 1), b)
            packed[q, j] = v
            return carry
        lax.fori_loop(0, half, body, 0, unroll=4)

    def in_remote(q, t):
        return remote(packed.at[q], est.at[0, block(t)], is_sem.at[q], ir_sem.at[t], "slab", q)

    def in_local(q, t):
        return pltpu.make_async_copy(packed.at[q], est.at[0, block(t)], ir_sem.at[t])

    group = (lane // rim) % (cols // rim)
    groups = cols // rim
    per = half // groups

    def pack_sides(load, put_left, put_right):
        for jj in range(per):
            v = [load(g * per + jj) for g in range(groups)]
            to_left, to_right = v[0], v[groups - 1]
            for g in range(1, groups):
                to_left = jnp.where(group == g, pltpu.roll(v[g], g * rim, 1), to_left)
            for g in range(groups - 1):
                to_right = jnp.where(group == g, pltpu.roll(v[g], LANES + (g + 1) * rim - cols, 1), to_right)
            put_left(jj, to_left)
            put_right(jj, to_right)

    def side_in(side):
        return left_in if side == 0 else right_in

    def first_remote(q, side, t):
        buf = right_out if side == 0 else left_out
        to = q + 1 if side == 0 else q - 1
        return remote(
            buf.at[0, q], side_in(side).at[0, t], gs_sem.at[q, side], hr_sem.at[0, t, side], "slab", to)

    def first_local(q, side, t):
        buf = right_out if side == 0 else left_out
        return pltpu.make_async_copy(buf.at[0, q], side_in(side).at[0, t], hr_sem.at[0, t, side])

    def sided(q):
        return [side for side in range(2) if 0 <= (q + 1 if side == 0 else q - 1) < slabs_n]

    fetches[0].wait()

    for q in blocks:
        pack(q)
    for q in blocks:
        def put_left(jj, v):
            left_out[0, q, jj] = v

        def put_right(jj, v):
            right_out[0, q, jj] = v
        pack_sides(lambda j: packed[q, j], put_left, put_right)

    def send_quarter(q):
        @pl.when(slab == q)
        def _():
            in_local(q, slab).start()
        @pl.when(slab != q)
        def _():
            in_remote(q, slab).start()
        for side in range(2):
            of = q - 1 if side == 0 else q + 1
            if 0 <= of < slabs_n:
                @pl.when(slab == q)
                def _():
                    first_local(of, side, slab).start()
                @pl.when(slab != q)
                def _():
                    first_remote(of, side, slab).start()

    near = sorted(blocks, key=lambda q: min(q, slabs_n - 1 - q), reverse=True)
    for q in near:
        send_quarter(q)

    for side in range(2):
        @pl.when(slab == (0 if side == 0 else slabs_n - 1))
        def _():
            side_in(side)[...] = jnp.zeros(side_in(side).shape, F32)
        @pl.when(row == (0 if side == 0 else rows_n - 1))
        def _():
            start = 0 if side == 0 else rim + height
            for e in range(2 * ITERS):
                ybuf[e, :, start:start + rim, :] = jnp.zeros((half * slabs_n, rim, LANES), F32)
    ends = half * (2 * slabs_n + 2)
    for buf in (bw, rw):
        buf[0:half] = jnp.zeros((half, height, LANES), F32)
        buf[ends:ends + half] = jnp.zeros((half, height, LANES), F32)

    for d in range(1, slabs_n):
        lines_copy(d, (slab + slabs_n - d) % slabs_n).wait_recv()

    in_row = lax.broadcasted_iota(jnp.int32, (LANES, 1), 0)
    same = (in_row // cols) == (lane // cols)

    def take(t, n, j):
        return lines[t, n, pl.ds(j, 1), :], lines[t, n, pl.ds(half + j, 1), :]

    def column_matrix(pair, j):
        both = jnp.concatenate([jnp.broadcast_to(line, (cols, LANES)) for line in pair], axis=0)
        main = jnp.where(same, pltpu.roll(both, LANES - radius, 1, stride=1, stride_axis=0), 0.0)
        rims = []
        for p, line in enumerate(pair):
            for side in range(2):
                shift = (p * cols + (cols if side else -rim) - radius) % LANES
                tile = pltpu.roll(jnp.broadcast_to(line, (rim, LANES)), shift, 1, stride=1, stride_axis=0)
                rims.append(jnp.where(lane // cols == p, tile, 0.0))
        part = jnp.concatenate([tile for tile in rims for _ in range(2)], axis=0)
        outer = jnp.where((in_row // rim) % 2 == (j // per) % 2, part, 0.0)
        return main, outer, rims

    def store_columns(w, zz, main, outer):
        for start, m in ((0, main), (LANES, outer)):
            high, low = split(m)
            w[zz, start:start + LANES, 0:LANES] = high
            w[zz, start:start + LANES, LANES:2 * LANES] = low

    def store_row_matrix(a_h, a_l, zz, a):
        high = a.astype(BF16).astype(F32)
        wide = jnp.concatenate([high, jnp.zeros(a.shape, F32)], axis=1)
        a_h[zz] = (wide + pltpu.roll(wide, reach, 1)).astype(BF16)
        a_l[zz] = (a - high).astype(BF16)

    def row_matrix(line):
        return pltpu.roll(
            jnp.broadcast_to(line, (height, LANES)), rim - radius, 1, stride=1, stride_axis=0)

    def build_forward(zz, carry):
        t, j = zz // half, zz % half
        main, outer, _ = column_matrix(take(t, 3, j), j)
        store_columns(wf, zz, main, outer)
        store_row_matrix(fh, fl, zz, jnp.concatenate([row_matrix(line) for line in take(t, 0, j)], axis=0))
        return carry

    at_row = row * height - rim + lane
    in_grid = (at_row >= 0) & (at_row < rows_n * height)

    def build_adjoint(zz, carry):
        t, j = zz // half, zz % half
        main, outer, rims = column_matrix(take(t, 2, j), j)
        tzv = jnp.zeros((1, LANES), F32)
        for k in range(taps):
            tzv = jnp.where(lane == k, tz_ref[k], tzv)
        cz = []
        for p in range(2):
            plane = t * depth + p * half + j + radius - lane
            inside = (plane >= 0) & (plane < slabs_n * depth)
            cz.append(jnp.sum(jnp.where(inside, tzv, 0.0), axis=1, keepdims=True))
        total = jnp.sum(main, axis=0, keepdims=True)
        for p in range(2):
            for side in range(2):
                there = (slab > 0) if side == 0 else (slab < slabs_n - 1)
                total = total + jnp.where(there, jnp.sum(rims[2 * p + side], axis=0, keepdims=True), 0.0)
        scale = 1.0 / (total * jnp.where(first_half, cz[0], cz[1]))
        store_columns(wa, zz, main * scale, outer * scale)
        parts = []
        for line in take(t, 1, j):
            a = row_matrix(line)
            parts.append(a / jnp.sum(jnp.where(in_grid, a, 0.0), axis=1, keepdims=True))
        store_row_matrix(ah, al, zz, jnp.concatenate(parts, axis=0))
        return carry

    def halo_copy(e, t, side):
        buf = right_out if side == 0 else left_out
        to = slab + 1 if side == 0 else slab - 1
        return remote(buf.at[e, t], side_in(side).at[e, t], hs_sem.at[e, t, side], hr_sem.at[e, t, side], "slab", to)

    has_send = (slab < slabs_n - 1, slab > 0)
    has_recv = (slab > 0, slab < slabs_n - 1)

    def share_sides(e, t, source):
        def put_left(jj, v):
            left_out[e, t, jj] = v

        def put_right(jj, v):
            right_out[e, t, jj] = v
        pack_sides(lambda j: source[half * t + j], put_left, put_right)
        for side in range(2):
            @pl.when(has_send[side])
            def _():
                halo_copy(e, t, side).start()

    def recv_sides(e, t):
        for side in range(2):
            @pl.when(has_recv[side])
            def _():
                if e > 0:
                    halo_copy(e, t, side).wait_recv()
                else:
                    first_wait(t, side)

    def first_wait(t, side):
        buf = right_out if side == 0 else left_out
        @pl.when(t == slab)
        def _():
            pltpu.make_async_copy(buf.at[0, 0], side_in(side).at[0, t], hr_sem.at[0, t, side]).wait()
        @pl.when(t != slab)
        def _():
            remote(buf.at[0, 0], side_in(side).at[0, t], gs_sem.at[0, side], hr_sem.at[0, t, side], "slab",
                   (slab + 1) % slabs_n).wait_recv()

    def in_wait(t):
        @pl.when(t == slab)
        def _():
            in_local(0, t).wait()
        @pl.when(t != slab)
        def _():
            remote(packed.at[0], est.at[0, block(t)], is_sem.at[0], ir_sem.at[t], "slab",
                   (slab + 1) % slabs_n).wait_recv()

    def row_copy(e, t, side):
        if side == 0:
            src_start, dst_start = height, 0
        else:
            src_start, dst_start = rim, rim + height
        return remote(
            ybuf.at[e, block(t), pl.ds(src_start, rim), :], ybuf.at[e, block(t), pl.ds(dst_start, rim), :],
            xs_sem.at[e, t, side], xr_sem.at[e, t, side], "row", beside[side][1])

    low_side = (lane // (2 * rim)) % 2 == 0

    def stage_y(e, t, source, w):
        recv_sides(e, t)
        for jj in range(per):
            l, r = left_in[e, t, jj], right_in[e, t, jj]
            edge[jj] = jnp.where(low_side, l, pltpu.roll(r, 2 * rim, 1))
            edge[per + jj] = jnp.where(low_side, pltpu.roll(l, LANES - 2 * rim, 1), r)

        def body(j, carry):
            zz = half * t + j
            v = jnp.concatenate([source[zz], edge[(j // (2 * per)) * per + j % per]], axis=1)
            high, low = split(v)
            both = jnp.dot(jnp.concatenate([high, low], axis=0), w[zz], preferred_element_type=F32)
            ybuf[e, zz, rim:rim + height, :] = (
                both[:height, :LANES] + both[height:, :LANES] + both[:height, LANES:])
            return carry
        lax.fori_loop(0, half, body, 0, unroll=UNROLL)
        for side in range(2):
            @pl.when(beside[side][0])
            def _():
                row_copy(e, t, side).start()

    def stage_x(e, t, a_h, a_l, put):
        for side in range(2):
            @pl.when(beside[1 - side][0])
            def _():
                row_copy(e, t, side).wait_recv()

        def body(j, carry):
            zz = half * t + j
            high, low = split(ybuf[e, zz])
            made = jnp.dot(a_h[zz][:, :2 * reach], jnp.concatenate([high, low], axis=0), preferred_element_type=F32)
            made = made + jnp.dot(a_l[zz][:, :reach], high, preferred_element_type=F32)
            put(t, j, jnp.where(first_half, made[:height], made[height:]))
            return carry
        lax.fori_loop(0, half, body, 0, unroll=UNROLL)

    def between(buf, t):
        def body(j, carry):
            at = depth * (t + 1) + j
            buf[at + half] = pltpu.roll(jnp.where(first_half, buf[at + depth], buf[at]), cols, 1)
            return carry
        lax.fori_loop(0, half, body, 0, unroll=4)

    def stage_z(buf, t, flip, put):
        def body(n, carry):
            tile = pl.ds(pl.multiple_of(n * 8, 8), 8)
            total = [None] * half
            for m in range(half + taps - 1):
                v = buf[depth * (t + 1) - radius + m, tile, :]
                for j in range(half):
                    k = m - j
                    if 0 <= k < taps:
                        term = tz_ref[taps - 1 - k if flip else k] * v
                        total[j] = term if total[j] is None else total[j] + term
            for j in range(half):
                put(t, j, tile, total[j])
            return carry
        lax.fori_loop(0, height // 8, body, 0)

    def put_blur(t, j, v):
        bw[depth * (t + 1) + j] = v

    def put_ratio(t, j, tile, v):
        rw[depth * (t + 1) + j, tile, :] = est[0, half * t + j, tile, :] / v

    def put_c(t, j, tile, v):
        cbuf[half * t + j, tile, :] = v

    def put_next(t, j, v):
        est[1, half * t + j] = est[0, half * t + j] * v

    def put_final(t, j, v):
        final[half * t + j] = est[1, half * t + j] * v

    def forward_y(it, t):
        stage_y(2 * it, t, est.at[it], wf)

    def forward_x(it, t):
        stage_x(2 * it, t, fh, fl, put_blur)

    def adjoint_y(it, t):
        stage_y(2 * it + 1, t, cbuf, wa)

    def adjoint_x(it, t):
        stage_x(2 * it + 1, t, ah, al, put_next if it == 0 else put_final)

    def ratio(t):
        stage_z(bw, t, False, put_ratio)

    def turn(it, t):
        stage_z(rw, t, True, put_c)
        share_sides(2 * it + 1, t, cbuf)

    last = slabs_n - 1

    def nth(i):
        return i + lower * (last - 2 * i)

    def mid(i):
        return i + lower * (last - 1 - 2 * i)

    first_end, last_end = -1 + lower * slabs_n, last - lower * slabs_n

    lax.fori_loop(0, half * slabs_n, build_forward, 0, unroll=2)
    for i in range(2):
        in_wait(nth(i))
        forward_y(0, nth(i))
    lax.fori_loop(0, half * slabs_n, build_adjoint, 0, unroll=2)
    for i in range(2):
        forward_x(0, nth(i))
    between(bw, first_end)
    between(bw, mid(0))
    ratio(nth(0))
    between(rw, first_end)
    for i in range(2, slabs_n):
        in_wait(nth(i))
        forward_y(0, nth(i))
        forward_x(0, nth(i))
        between(bw, mid(i - 1))
        ratio(nth(i - 1))
        between(rw, mid(i - 2))
        turn(0, nth(i - 2))
    between(bw, last_end)
    ratio(nth(last))
    between(rw, mid(last - 1))
    between(rw, last_end)
    turn(0, nth(last - 1))
    turn(0, nth(last))

    inner = list(range(1, slabs_n - 1)) + [0, last]

    def lagged(first, second, seq):
        for n, t in enumerate(seq):
            first(t)
            if n > 0:
                second(seq[n - 1])
        second(seq[-1])

    def next_x(t):
        adjoint_x(0, t)
        share_sides(2, t, est.at[1])

    lagged(functools.partial(adjoint_y, 0), next_x, inner)
    lagged(functools.partial(forward_y, 1), functools.partial(forward_x, 1), inner)

    for t in range(-1, slabs_n):
        between(bw, t)
    outer = []
    for n in range(slabs_n // 2):
        outer += [last - n, n]
    done = set()

    def need(t):
        if 0 <= t < slabs_n and t not in done:
            done.add(t)
            ratio(t)
    joined = set()
    for t in outer:
        for s in (t, t - 1, t + 1):
            need(s)
        for s in (t - 1, t):
            if s not in joined:
                joined.add(s)
                between(rw, s)
        turn(1, t)

    def out_remote(t, q):
        return remote(final.at[block(t)], back.at[q], os_sem.at[t], or_sem.at[q], "slab", t)

    def out_local(t, q):
        return pltpu.make_async_copy(final.at[block(t)], back.at[q], or_sem.at[q])

    def last_x(t):
        adjoint_x(1, t)
        @pl.when(slab == t)
        def _():
            out_local(t, slab).start()
        @pl.when(slab != t)
        def _():
            out_remote(t, slab).start()

    lagged(functools.partial(adjoint_y, 1), last_x, outer)

    for q in blocks:
        @pl.when(slab == q)
        def _():
            out_local(0, q).wait()
        @pl.when(slab != q)
        def _():
            remote(final.at[block(0)], back.at[q], os_sem.at[0], or_sem.at[q], "slab", (slab + 1) % slabs_n).wait_recv()

    def unpack(j, carry):
        for b in range(width // LANES):
            x, y = back[2 * b, j], back[2 * b + 1, j]
            out_ref[j, :, b * LANES:(b + 1) * LANES] = jnp.where(first_half, x, pltpu.roll(y, cols, 1))
            out_ref[half + j, :, b * LANES:(b + 1) * LANES] = jnp.where(first_half, pltpu.roll(x, cols, 1), y)
        return carry
    lax.fori_loop(0, half, unpack, 0, unroll=2)

    for d in range(1, slabs_n):
        lines_copy(d, slab).wait_send()
    for q in blocks:
        @pl.when(slab != q)
        def _():
            in_remote(q, slab).wait_send()
            out_remote(q, slab).wait_send()
        for side in range(2):
            of = q - 1 if side == 0 else q + 1
            if 0 <= of < slabs_n:
                @pl.when(slab != q)
                def _():
                    first_remote(of, side, slab).wait_send()
    for e in range(2 * ITERS):
        for t in blocks:
            for side in range(2):
                if e > 0:
                    @pl.when(has_send[side])
                    def _():
                        halo_copy(e, t, side).wait_send()
                @pl.when(beside[side][0])
                def _():
                    row_copy(e, t, side).wait_send()


def reshards(depth, height, width, taps, slabs_n):
    return (
        slabs_n >= 2 and width == slabs_n * (LANES // 2) and depth % (2 * (LANES // 2 // CHUNK)) == 0
        and height % CHUNK == 0 and height + 2 * CHUNK <= LANES - CHUNK and taps // 2 < CHUNK
        and depth * slabs_n * height <= 4096
    )


def fast_call(observed, taps_x, rows_n, slabs_n):
    depth, height, width = observed.shape
    bands, taps = taps_x.shape
    half = depth // 2
    planes = half * slabs_n
    reach = height + 2 * CHUNK
    per = half // (LANES // 2 // CHUNK)
    exchanges = 2 * ITERS
    vmem = pl.BlockSpec(memory_space=pltpu.VMEM)
    hbm = pl.BlockSpec(memory_space=pltpu.HBM)
    sides = pltpu.VMEM((exchanges, slabs_n, per, height, LANES), F32)
    dma = pltpu.SemaphoreType.DMA
    return pl.pallas_call(
        functools.partial(fast_kernel, rows_n, slabs_n, taps),
        out_shape=jax.ShapeDtypeStruct(observed.shape, F32),
        in_specs=[hbm] * 5,
        out_specs=vmem,
        scratch_shapes=[
            pltpu.SMEM((depth,), jnp.int32),
            pltpu.SMEM((taps,), F32),
            pltpu.VMEM((bands, taps), F32),
            pltpu.VMEM((bands, taps), F32),
            dma((5,)),
        ] + [pltpu.VMEM((bands, LANES), F32)] * 4 + [
            pltpu.VMEM((slabs_n, 4, depth, LANES), F32),
            pltpu.VMEM((depth, height, width), F32),
            pltpu.VMEM((slabs_n, half, height, LANES), F32),
            pltpu.VMEM((ITERS, planes, height, LANES), F32),
            pltpu.VMEM((planes, height, LANES), F32),
            pltpu.VMEM((slabs_n, half, height, LANES), F32),
            pltpu.VMEM((exchanges, planes, reach, LANES), F32),
            sides, sides, sides, sides,
            pltpu.VMEM((2 * per, height, LANES), F32),
            pltpu.VMEM((planes, 2 * LANES, 2 * LANES), BF16),
            pltpu.VMEM((planes, 2 * LANES, 2 * LANES), BF16),
            pltpu.VMEM((planes, 2 * height, 2 * LANES), BF16),
            pltpu.VMEM((planes, 2 * height, LANES), BF16),
            pltpu.VMEM((planes, 2 * height, 2 * LANES), BF16),
            pltpu.VMEM((planes, 2 * height, LANES), BF16),
            pltpu.VMEM((2 * planes + 3 * half, height, LANES), F32),
            pltpu.VMEM((2 * planes + 3 * half, height, LANES), F32),
            pltpu.VMEM((planes, height, LANES), F32),
            dma((slabs_n - 1,)), dma((slabs_n,)),
            dma((slabs_n,)), dma((slabs_n,)), dma((slabs_n, 2)),
            dma((exchanges, slabs_n, 2)), dma((exchanges, slabs_n, 2)),
            dma((exchanges, slabs_n, 2)), dma((exchanges, slabs_n, 2)),
            dma((slabs_n,)), dma((slabs_n,)),
        ],
        compiler_params=pltpu.CompilerParams(
            collective_id=0, has_side_effects=True, vmem_limit_bytes=63 * 1024 * 1024
        ),
    )


def solution(mesh):
    rows_n, slabs_n = mesh.shape["row"], mesh.shape["slab"]

    def on_device(observed, band_index, taps_x, taps_y, taps_z):
        depth, height, width = observed.shape
        bands, taps = taps_x.shape
        radius = taps // 2
        if reshards(depth, height, width, taps, slabs_n):
            return fast_call(observed, taps_x, rows_n, slabs_n)(band_index, taps_z, taps_x, taps_y, observed)

        vmem = pl.BlockSpec(memory_space=pltpu.VMEM)
        hbm = pl.BlockSpec(memory_space=pltpu.HBM)
        chunks = height // CHUNK
        return pl.pallas_call(
            functools.partial(kernel, rows_n, slabs_n, taps),
            out_shape=jax.ShapeDtypeStruct(observed.shape, F32),
            in_specs=[hbm] * 5,
            out_specs=vmem,
            scratch_shapes=[
                pltpu.SMEM((depth,), jnp.int32),
                pltpu.SMEM((taps,), F32),
                pltpu.VMEM((bands, taps), F32),
                pltpu.VMEM((bands, taps), F32),
                pltpu.SemaphoreType.DMA((5,)),
            ] + [pltpu.VMEM((bands, LANES), F32)] * 4 + [
                pltpu.VMEM((ITERS, depth, height + 2 * CHUNK, width), F32),
                pltpu.VMEM((ITERS, depth, height + 2 * CHUNK, width), F32),
                pltpu.VMEM((ITERS, depth + 2 * radius, height, width), F32),
                pltpu.VMEM((ITERS, depth + 2 * radius, height, width), F32),
                pltpu.VMEM((depth, width, width), BF16),
                pltpu.VMEM((depth, width, width), BF16),
                pltpu.VMEM((depth, width, width), BF16),
                pltpu.VMEM((depth, width, width), BF16),
                pltpu.VMEM((depth, CHUNK, width), BF16),
                pltpu.VMEM((depth, chunks, CHUNK, width), BF16),
                pltpu.SemaphoreType.DMA((ITERS, 2, chunks, 2)),
                pltpu.SemaphoreType.DMA((ITERS, 2, chunks, 2)),
                pltpu.SemaphoreType.DMA((ITERS, 2, 2)),
                pltpu.SemaphoreType.DMA((ITERS, 2, 2)),
            ],
            compiler_params=pltpu.CompilerParams(
                collective_id=0, has_side_effects=True, vmem_limit_bytes=63 * 1024 * 1024 + 900 * 1024
            ),
        )(
            band_index, taps_z, taps_x, taps_y,
            observed,
        )

    in_specs = (P(("grp", "slab"), "row", None), P("slab"), P(), P(), P())
    return jax.shard_map(
        on_device, mesh=mesh, in_specs=in_specs, out_specs=P(("grp", "slab"), "row", None), check_vma=False
    )
```

```python
import functools

import jax
import jax.numpy as jnp
from jax import lax
from jax.experimental import pallas as pl
from jax.experimental.pallas import tpu as pltpu
from jax.sharding import PartitionSpec as P

ITERS = 2
CHUNK = 16
LANES = 128
GROUP = 8
PASSES = 1
F32 = jnp.float32
BF16 = jnp.bfloat16


def split(v):
    high = v.astype(BF16)
    return high, (v - high.astype(F32)).astype(BF16)


def chunk_order(count, it):
    first = [1, 0] if it == 0 else [0, 1]
    inner = list(range(2, count - 1))
    return first + ([count - 1] + inner if it == ITERS - 1 else inner + [count - 1])


def kernel(
    rows_n, slabs_n, taps,
    band_hbm, tz_hbm, tx_hbm, ty_hbm, obs_hbm,
    out_ref,
    band_ref, tz_ref, tx_ref, ty_ref, in_sem,
    txf_ref, txr_ref, tyf_ref, tyr_ref, ext, dext, bz, rz, wf, wa, scale, af, aa, mid,
    zs_sem, zr_sem, xs_sem, xr_sem,
):
    depth, height, width = obs_hbm.shape
    radius = taps // 2
    halo = CHUNK
    chunks = height // CHUNK
    row = lax.axis_index("row")
    slab = lax.axis_index("slab")
    parity = row % 2

    def chunk(p):
        return p + parity * (chunks - 1 - 2 * p)

    def begin(p, more=0, unit=CHUNK):
        return pl.multiple_of(chunk(p) * CHUNK + more, unit)

    fetches = [
        pltpu.make_async_copy(src, dst, in_sem.at[n])
        for n, (src, dst) in enumerate((
            (obs_hbm, ext.at[0, :, pl.ds(halo, height), :]),
            (ty_hbm, ty_ref), (tx_hbm, tx_ref), (band_hbm, band_ref), (tz_hbm, tz_ref),
        ))
    ]
    for fetch in fetches:
        fetch.start()

    sides = {
        ("row", 0): (row < rows_n - 1, row + 1),
        ("row", 1): (row > 0, row - 1),
        ("slab", 0): (slab < slabs_n - 1, slab + 1),
        ("slab", 1): (slab > 0, slab - 1),
    }

    barrier = pltpu.get_barrier_semaphore()
    for (axis, _), (there, index) in sides.items():
        @pl.when(there)
        def _(axis=axis, index=index):
            pl.semaphore_signal(barrier, inc=1, device_id={axis: index}, device_id_type=pl.DeviceIdType.MESH)

    def clear(axis, buffer, it):
        for side in range(2):
            @pl.when(jnp.logical_not(sides[(axis, side)][0]))
            def _():
                if axis == "row":
                    first = 0 if side == 1 else halo + height
                    buffer[it, :, first:first + halo, :] = jnp.zeros((depth, halo, width), F32)
                else:
                    first = 0 if side == 1 else radius + depth
                    buffer[it, first:first + radius] = jnp.zeros((radius, height, width), F32)

    pl.semaphore_wait(barrier, sum(there.astype(jnp.int32) for there, _ in sides.values()))

    def row_copy(src, dst, it, which, side):
        if side == 0:
            src_start, dst_start = src[1] + height - halo, 0
        else:
            src_start, dst_start = src[1], halo + height
        return pltpu.make_async_remote_copy(
            src_ref=src[0].at[:, pl.ds(src_start, halo), :],
            dst_ref=dst.at[it, :, pl.ds(dst_start, halo), :],
            send_sem=xs_sem.at[it, which, side],
            recv_sem=xr_sem.at[it, which, side],
            device_id={"row": sides[("row", side)][1]},
            device_id_type=pl.DeviceIdType.MESH,
        )

    def slab_copy(buf, it, which, c, side):
        if side == 0:
            src_start, dst_start = depth, 0
        else:
            src_start, dst_start = radius, radius + depth
        span = pl.ds(begin(c), CHUNK)
        return pltpu.make_async_remote_copy(
            src_ref=buf.at[it, pl.ds(src_start, radius), span, :],
            dst_ref=buf.at[it, pl.ds(dst_start, radius), span, :],
            send_sem=zs_sem.at[it, which, c, side],
            recv_sem=zr_sem.at[it, which, c, side],
            device_id={"slab": sides[("slab", side)][1]},
            device_id_type=pl.DeviceIdType.MESH,
        )

    def start(axis, side, make, also=True):
        @pl.when(sides[(axis, side)][0] & also)
        def _():
            make(side).start()

    def recv(axis, side, make, also=True):
        @pl.when(sides[(axis, 1 - side)][0] & also)
        def _():
            make(side).wait_recv()

    def sent(axis, side, make):
        @pl.when(sides[(axis, side)][0])
        def _():
            make(side).wait_send()

    sends = []

    def x_make(it, which):
        buffer = ext if which == 0 else dext
        return functools.partial(row_copy, (buffer.at[it], halo), buffer, it, which)

    def z_make(it, which, c):
        return functools.partial(slab_copy, bz if which == 0 else rz, it, which, c)

    def x_start(it, which, p):
        near = p == 0
        for v in range(2):
            side = 1 - v if near else v
            start("row", side, x_make(it, which), parity == v)
        if near:
            sends.extend(("row", side, x_make(it, which)) for side in range(2))

    def x_recv(it, which, p):
        near = p == 0
        for v in range(2):
            recv("row", v if near else 1 - v, x_make(it, which), parity == v)

    def z_start(it, which, c):
        for side in range(2):
            start("slab", side, z_make(it, which, c))
            sends.append(("slab", side, z_make(it, which, c)))

    def z_recv(it, which, c):
        for side in range(2):
            recv("slab", side, z_make(it, which, c))

    fetches[0].wait()
    for p in (0, chunks - 1):
        x_start(0, 0, p)
    for fetch in fetches[1:]:
        fetch.wait()

    kk = 3 * halo
    mirror = (
        lax.broadcasted_iota(jnp.int32, (LANES, LANES), 0) + lax.broadcasted_iota(jnp.int32, (LANES, LANES), 1)
        == taps - 1
    ).astype(F32)
    for source, ahead, back in ((tx_ref, txf_ref, txr_ref), (ty_ref, tyf_ref, tyr_ref)):
        ahead[...] = jnp.zeros(ahead.shape, F32)
        ahead[:, 0:taps] = source[...]
        back[...] = jnp.dot(ahead[...], mirror, precision=lax.Precision.HIGHEST, preferred_element_type=F32)

    lane = lax.broadcasted_iota(jnp.int32, (1, LANES), 1)
    blocks = range(width // LANES)

    def column_band(line):
        gap = lax.broadcasted_iota(jnp.int32, (LANES, LANES), 0) - lane
        ring = pltpu.roll(jnp.broadcast_to(line, (LANES, LANES)), LANES - radius, 1, stride=1, stride_axis=0)
        main = jnp.where((gap <= radius) & (gap >= -radius), ring, 0.0)
        short = jnp.broadcast_to(line, (halo, LANES))
        after = pltpu.roll(short, LANES - radius, 1, stride=1, stride_axis=0)
        after = jnp.where(lane >= LANES - radius, after, 0.0)
        before = pltpu.roll(short, LANES - halo - radius, 1, stride=1, stride_axis=0)
        before = jnp.where(lane < radius, before, 0.0)
        return main, after, before

    def store_band(w, z, band):
        for start, part in zip((0, LANES, LANES + halo), band):
            high, low = split(part)
            w[z, start:start + part.shape[0], 0:LANES] = high
            w[z, start:start + part.shape[0], LANES:2 * LANES] = low

    def store_rows(a):
        high = a.astype(BF16).astype(F32)
        low = a - high
        zero = jnp.zeros(a.shape, F32)
        first = jnp.concatenate([high, zero], axis=1)
        second = jnp.concatenate([low, zero], axis=1)
        return (first + pltpu.roll(second, kk, 1) + pltpu.roll(first, 2 * kk, 1)).astype(BF16)

    def row_band(line):
        return pltpu.roll(jnp.broadcast_to(line, (CHUNK, LANES)), halo - radius, 1, stride=1, stride_axis=0)

    def build_forward(z, carry):
        at = pl.ds(band_ref[z], 1)
        store_band(wf, z, column_band(tyr_ref[at, :]))
        af[z] = store_rows(row_band(txf_ref[at, :]))
        return carry

    def build_adjoint(z, carry):
        at = pl.ds(band_ref[z], 1)
        band = column_band(tyf_ref[at, :])
        store_band(wa, z, band)
        tzv = jnp.zeros((1, LANES), F32)
        for k in range(taps):
            tzv = jnp.where(lane == k, tz_ref[k], tzv)
        plane = slab * depth + z + radius - lane
        inside = (plane >= 0) & (plane < slabs_n * depth)
        cz = jnp.sum(jnp.where(inside, tzv, 0.0), axis=1, keepdims=True)
        main, after, before = [jnp.sum(part, axis=0, keepdims=True) for part in band]
        for j in blocks:
            total = main
            if j > 0:
                total = total + before
            if j < blocks[-1]:
                total = total + after
            scale[z, :, j * LANES:(j + 1) * LANES] = 1.0 / (total * cz)
        base = row_band(txr_ref[at, :])
        for c in range(chunks):
            at_row = row * height + (c - 1) * CHUNK + lax.broadcasted_iota(jnp.int32, (CHUNK, LANES), 1)
            inside = (at_row >= 0) & (at_row < rows_n * height)
            aa[z, c] = store_rows(base / jnp.sum(jnp.where(inside, base, 0.0), axis=1, keepdims=True))
        return carry

    def blur_rows(a, v):
        high, low = split(v)
        return jnp.dot(a[:, :3 * kk], jnp.concatenate([high, high, low], axis=0), preferred_element_type=F32)

    def blur_columns(v, w):
        n = v.shape[0]
        parts = [v[:, b * LANES:(b + 1) * LANES] for b in blocks]
        wide = []
        for b in blocks:
            outer = jnp.zeros((n, LANES), F32)
            if b > 0:
                outer = jnp.where(lane < 2 * halo, pltpu.roll(parts[b - 1], 2 * halo, 1), outer)
            outer = jnp.where(lane < halo, parts[b + 1] if b < blocks[-1] else 0.0, outer)
            wide.append(jnp.concatenate([parts[b], outer], axis=1))
        wide = jnp.concatenate(split(jnp.concatenate(wide, axis=0)), axis=0)
        both = jnp.dot(wide[:, :LANES + 2 * halo], w, preferred_element_type=F32)
        m = n * len(blocks)
        made = both[:m, :LANES] + both[m:, :LANES] + both[:m, LANES:]
        return jnp.concatenate([made[b * n:(b + 1) * n] for b in blocks], axis=1)

    def edge(it, which, p):
        if p in (0, chunks - 1):
            x_recv(it, which, p)

    def planes(make, put):
        def body(n, carry):
            made = [make(n * GROUP + i) for i in range(GROUP)]
            for i, v in enumerate(made):
                put(n * GROUP + i, v)
            return carry
        lax.fori_loop(0, depth // GROUP, body, 0, unroll=PASSES)

    def stage_xy(it, p):
        edge(it, 0, p)
        c = begin(p)

        def make(z):
            return blur_columns(blur_rows(af[z], ext[it, z, pl.ds(c, kk), :]), wf[z])

        def put(z, v):
            bz[it, radius + z, pl.ds(c, CHUNK), :] = v
        planes(make, put)
        z_start(it, 0, p)

    def blur_depth(buf, it, tile, lanes, flip):
        total = None
        for k in range(taps):
            weight = tz_ref[taps - 1 - k] if flip else tz_ref[k]
            term = weight * buf[it, k:k + depth, tile, lanes]
            total = term if total is None else total + term
        return total

    def tiles(p):
        for r in range(0, CHUNK, 8):
            for l in range(0, width, LANES):
                yield pl.ds(begin(p, r, 8), 8), pl.ds(begin(p, halo + r, 8), 8), slice(l, l + LANES)

    def stage_ratio(it, p):
        for tile, inner, lanes in tiles(p):
            blurred = blur_depth(bz, it, tile, lanes, False)
            rz[it, radius:radius + depth, tile, lanes] = ext[0, :, inner, lanes] / blurred
        z_start(it, 1, p)

    def stage_zy(it, p):
        for r in range(0, CHUNK, 8):
            for l in range(0, width, LANES):
                lanes = slice(l, l + LANES)
                mid[:, r:r + 8, lanes] = blur_depth(rz, it, pl.ds(begin(p, r, 8), 8), lanes, True)
        rows = pl.ds(begin(p, halo), CHUNK)

        def put(z, v):
            dext[it, z, rows, :] = v
        planes(lambda z: blur_columns(mid[z], wa[z]) * scale[z], put)
        if p in (0, chunks - 1):
            x_start(it, 1, p)

    def stage_x(it, p):
        edge(it, 1, p)
        c = begin(p)
        inner = pl.ds(begin(p, halo), CHUNK)

        def make(z):
            return ext[it, z, inner, :] * blur_rows(aa[z, chunk(p)], dext[it, z, pl.ds(c, kk), :])

        def put(z, v):
            if it == ITERS - 1:
                out_ref[z, pl.ds(c, CHUNK), :] = v
            else:
                ext[it + 1, z, inner, :] = v
        planes(make, put)
        if it < ITERS - 1 and p in (0, chunks - 1):
            x_start(it + 1, 0, p)

    clear("row", ext, 0)
    lax.fori_loop(0, depth, build_forward, 0, unroll=2)
    started = 0
    for it in range(ITERS):
        order = chunk_order(chunks, it)
        for p in order[started:]:
            stage_xy(it, p)
        if it == 0:
            lax.fori_loop(0, depth, build_adjoint, 0)
            for buffer in (bz, rz):
                for i in range(ITERS):
                    clear("slab", buffer, i)
            for i in range(ITERS):
                clear("row", dext, i)
            for i in range(1, ITERS):
                clear("row", ext, i)
        for p in order:
            z_recv(it, 0, p)
            stage_ratio(it, p)
        for p in order[:-1]:
            z_recv(it, 1, p)
            stage_zy(it, p)
        if it < ITERS - 1:
            for p in range(chunks - 2):
                stage_x(it, p)
            for p in range(chunks - 3):
                stage_xy(it + 1, p)
            z_recv(it, 1, order[-1])
            stage_zy(it, order[-1])
            stage_x(it, chunks - 2)
            stage_xy(it + 1, chunks - 3)
            stage_x(it, chunks - 1)
            started = chunks - 2
        else:
            early = [p for p in range(chunks) if abs(p - order[-1]) > 1]
            for p in early:
                stage_x(it, p)
            z_recv(it, 1, order[-1])
            stage_zy(it, order[-1])
            for p in range(chunks):
                if p not in early:
                    stage_x(it, p)

    for axis, side, make in sends:
        sent(axis, side, make)


def solution(mesh):
    rows_n, slabs_n = mesh.shape["row"], mesh.shape["slab"]

    def on_device(observed, band_index, taps_x, taps_y, taps_z):
        depth, height, width = observed.shape
        bands, taps = taps_x.shape
        radius = taps // 2

        vmem = pl.BlockSpec(memory_space=pltpu.VMEM)
        hbm = pl.BlockSpec(memory_space=pltpu.HBM)
        chunks = height // CHUNK
        return pl.pallas_call(
            functools.partial(kernel, rows_n, slabs_n, taps),
            out_shape=jax.ShapeDtypeStruct(observed.shape, F32),
            in_specs=[hbm] * 5,
            out_specs=vmem,
            scratch_shapes=[
                pltpu.SMEM((depth,), jnp.int32),
                pltpu.SMEM((taps,), F32),
                pltpu.VMEM((bands, taps), F32),
                pltpu.VMEM((bands, taps), F32),
                pltpu.SemaphoreType.DMA((5,)),
            ] + [pltpu.VMEM((bands, LANES), F32)] * 4 + [
                pltpu.VMEM((ITERS, depth, height + 2 * CHUNK, width), F32),
                pltpu.VMEM((ITERS, depth, height + 2 * CHUNK, width), F32),
                pltpu.VMEM((ITERS, depth + 2 * radius, height, width), F32),
                pltpu.VMEM((ITERS, depth + 2 * radius, height, width), F32),
                pltpu.VMEM((depth, LANES + 2 * CHUNK, 2 * LANES), BF16),
                pltpu.VMEM((depth, LANES + 2 * CHUNK, 2 * LANES), BF16),
                pltpu.VMEM((depth, 1, width), F32),
                pltpu.VMEM((depth, CHUNK, 2 * LANES), BF16),
                pltpu.VMEM((depth, chunks, CHUNK, 2 * LANES), BF16),
                pltpu.VMEM((depth, CHUNK, width), F32),
                pltpu.SemaphoreType.DMA((ITERS, 2, chunks, 2)),
                pltpu.SemaphoreType.DMA((ITERS, 2, chunks, 2)),
                pltpu.SemaphoreType.DMA((ITERS, 2, 2)),
                pltpu.SemaphoreType.DMA((ITERS, 2, 2)),
            ],
            compiler_params=pltpu.CompilerParams(
                collective_id=0, has_side_effects=True, vmem_limit_bytes=63 * 1024 * 1024 + 900 * 1024
            ),
        )(
            band_index, taps_z, taps_x, taps_y,
            observed,
        )

    in_specs = (P(("grp", "slab"), "row", None), P("slab"), P(), P(), P())
    return jax.shard_map(
        on_device, mesh=mesh, in_specs=in_specs, out_specs=P(("grp", "slab"), "row", None), check_vma=False
    )
```

```python
import functools

import jax
import jax.numpy as jnp
from jax import lax
from jax.experimental import pallas as pl
from jax.experimental.pallas import tpu as pltpu
from jax.sharding import PartitionSpec as P

ITERS = 2
CHUNK = 16
LANES = 128
GROUP = 8
PASSES = 1
F32 = jnp.float32
BF16 = jnp.bfloat16


def split(v):
    high = v.astype(BF16)
    return high, (v - high.astype(F32)).astype(BF16)


def chunk_order(count, it):
    first = [1, 0] if it == 0 else [0, 1]
    inner = list(range(2, count - 1))
    return first + ([count - 1] + inner if it == ITERS - 1 else inner + [count - 1])


def kernel(
    rows_n, slabs_n, taps,
    band_hbm, tz_hbm, tx_hbm, ty_hbm, obs_hbm,
    out_ref,
    band_ref, tz_ref, tx_ref, ty_ref, in_sem,
    txf_ref, txr_ref, tyf_ref, tyr_ref, ext, dext, bz, rz, wf, wa, scale, af, aa, ar, mid,
    zs_sem, zr_sem, xs_sem, xr_sem,
):
    depth, height, width = obs_hbm.shape
    radius = taps // 2
    halo = CHUNK
    chunks = height // CHUNK
    row = lax.axis_index("row")
    slab = lax.axis_index("slab")
    parity = row % 2

    def chunk(p):
        return p + parity * (chunks - 1 - 2 * p)

    def begin(p, more=0, unit=CHUNK):
        return pl.multiple_of(chunk(p) * CHUNK + more, unit)

    fetches = [
        pltpu.make_async_copy(src, dst, in_sem.at[n])
        for n, (src, dst) in enumerate((
            (obs_hbm, ext.at[0, :, pl.ds(halo, height), :]),
            (ty_hbm, ty_ref), (tx_hbm, tx_ref), (band_hbm, band_ref), (tz_hbm, tz_ref),
        ))
    ]
    for fetch in fetches:
        fetch.start()

    sides = {
        ("row", 0): (row < rows_n - 1, row + 1),
        ("row", 1): (row > 0, row - 1),
        ("slab", 0): (slab < slabs_n - 1, slab + 1),
        ("slab", 1): (slab > 0, slab - 1),
    }

    barrier = pltpu.get_barrier_semaphore()
    for (axis, _), (there, index) in sides.items():
        @pl.when(there)
        def _(axis=axis, index=index):
            pl.semaphore_signal(barrier, inc=1, device_id={axis: index}, device_id_type=pl.DeviceIdType.MESH)

    def clear(axis, buffer, it):
        for side in range(2):
            @pl.when(jnp.logical_not(sides[(axis, side)][0]))
            def _():
                if axis == "row":
                    first = 0 if side == 1 else halo + height
                    buffer[it, :, first:first + halo, :] = jnp.zeros((depth, halo, width), F32)
                else:
                    first = 0 if side == 1 else radius + depth
                    buffer[it, first:first + radius] = jnp.zeros((radius, height, width), F32)

    def row_copy(src, dst, it, which, side):
        if side == 0:
            src_start, dst_start = src[1] + height - halo, 0
        else:
            src_start, dst_start = src[1], halo + height
        return pltpu.make_async_remote_copy(
            src_ref=src[0].at[:, pl.ds(src_start, halo), :],
            dst_ref=dst.at[it, :, pl.ds(dst_start, halo), :],
            send_sem=xs_sem.at[it, which, side],
            recv_sem=xr_sem.at[it, which, side],
            device_id={"row": sides[("row", side)][1]},
            device_id_type=pl.DeviceIdType.MESH,
        )

    def slab_copy(buf, it, which, c, side):
        if side == 0:
            src_start, dst_start = depth, 0
        else:
            src_start, dst_start = radius, radius + depth
        span = pl.ds(begin(c), CHUNK)
        return pltpu.make_async_remote_copy(
            src_ref=buf.at[it, pl.ds(src_start, radius), span, :],
            dst_ref=buf.at[it, pl.ds(dst_start, radius), span, :],
            send_sem=zs_sem.at[it, which, c, side],
            recv_sem=zr_sem.at[it, which, c, side],
            device_id={"slab": sides[("slab", side)][1]},
            device_id_type=pl.DeviceIdType.MESH,
        )

    def start(axis, side, make, also=True):
        @pl.when(sides[(axis, side)][0] & also)
        def _():
            make(side).start()

    def recv(axis, side, make, also=True):
        @pl.when(sides[(axis, 1 - side)][0] & also)
        def _():
            make(side).wait_recv()

    def sent(axis, side, make):
        @pl.when(sides[(axis, side)][0])
        def _():
            make(side).wait_send()

    sends = []

    def x_make(it, which):
        buffer = ext if which == 0 else dext
        return functools.partial(row_copy, (buffer.at[it], halo), buffer, it, which)

    def z_make(it, which, c):
        return functools.partial(slab_copy, bz if which == 0 else rz, it, which, c)

    def x_start(it, which, p):
        near = p == 0
        for v in range(2):
            side = 1 - v if near else v
            start("row", side, x_make(it, which), parity == v)
        if near:
            sends.extend(("row", side, x_make(it, which)) for side in range(2))

    def x_recv(it, which, p):
        near = p == 0
        for v in range(2):
            recv("row", v if near else 1 - v, x_make(it, which), parity == v)

    def z_start(it, which, c):
        for side in range(2):
            start("slab", side, z_make(it, which, c))
            sends.append(("slab", side, z_make(it, which, c)))

    def z_recv(it, which, c):
        for side in range(2):
            recv("slab", side, z_make(it, which, c))

    for fetch in fetches[1:]:
        fetch.wait()

    kk = 3 * halo
    rest = height - CHUNK
    rest_begin = pl.multiple_of((1 - parity) * CHUNK, CHUNK)
    rk = rest + 2 * halo
    mirror = (
        lax.broadcasted_iota(jnp.int32, (LANES, LANES), 0) + lax.broadcasted_iota(jnp.int32, (LANES, LANES), 1)
        == taps - 1
    ).astype(F32)
    for source, ahead, back in ((tx_ref, txf_ref, txr_ref), (ty_ref, tyf_ref, tyr_ref)):
        ahead[...] = jnp.zeros(ahead.shape, F32)
        ahead[:, 0:taps] = source[...]
        back[...] = jnp.dot(ahead[...], mirror, precision=lax.Precision.HIGHEST, preferred_element_type=F32)

    lane = lax.broadcasted_iota(jnp.int32, (1, LANES), 1)
    blocks = range(width // LANES)

    def column_band(line):
        gap = lax.broadcasted_iota(jnp.int32, (LANES, LANES), 0) - lane
        ring = pltpu.roll(jnp.broadcast_to(line, (LANES, LANES)), LANES - radius, 1, stride=1, stride_axis=0)
        main = jnp.where((gap <= radius) & (gap >= -radius), ring, 0.0)
        short = jnp.broadcast_to(line, (halo, LANES))
        after = pltpu.roll(short, LANES - radius, 1, stride=1, stride_axis=0)
        after = jnp.where(lane >= LANES - radius, after, 0.0)
        before = pltpu.roll(short, LANES - halo - radius, 1, stride=1, stride_axis=0)
        before = jnp.where(lane < radius, before, 0.0)
        return main, after, before

    def store_band(w, z, band):
        for start, part in zip((0, LANES, LANES + halo), band):
            high, low = split(part)
            w[z, start:start + part.shape[0], 0:LANES] = high
            w[z, start:start + part.shape[0], LANES:2 * LANES] = low

    def store_rows(a):
        high = a.astype(BF16).astype(F32)
        low = a - high
        zero = jnp.zeros(a.shape, F32)
        first = jnp.concatenate([high, zero], axis=1)
        second = jnp.concatenate([low, zero], axis=1)
        return (first + pltpu.roll(second, kk, 1) + pltpu.roll(first, 2 * kk, 1)).astype(BF16)

    def row_band(line):
        return pltpu.roll(jnp.broadcast_to(line, (CHUNK, LANES)), halo - radius, 1, stride=1, stride_axis=0)

    def build_forward(z, carry):
        at = pl.ds(band_ref[z], 1)
        store_band(wf, z, column_band(tyr_ref[at, :]))
        af[z] = store_rows(row_band(txf_ref[at, :]))
        return carry

    def build_adjoint(z, carry):
        at = pl.ds(band_ref[z], 1)
        band = column_band(tyf_ref[at, :])
        store_band(wa, z, band)
        tzv = jnp.zeros((1, LANES), F32)
        for k in range(taps):
            tzv = jnp.where(lane == k, tz_ref[k], tzv)
        plane = slab * depth + z + radius - lane
        inside = (plane >= 0) & (plane < slabs_n * depth)
        cz = jnp.sum(jnp.where(inside, tzv, 0.0), axis=1, keepdims=True)
        main, after, before = [jnp.sum(part, axis=0, keepdims=True) for part in band]
        for j in blocks:
            total = main
            if j > 0:
                total = total + before
            if j < blocks[-1]:
                total = total + after
            scale[z, :, j * LANES:(j + 1) * LANES] = 1.0 / (total * cz)
        base = row_band(txr_ref[at, :])
        for c in range(chunks):
            at_row = row * height + (c - 1) * CHUNK + lax.broadcasted_iota(jnp.int32, (CHUNK, LANES), 1)
            inside = (at_row >= 0) & (at_row < rows_n * height)
            aa[z, c] = store_rows(base / jnp.sum(jnp.where(inside, base, 0.0), axis=1, keepdims=True))
        long = pltpu.roll(
            jnp.broadcast_to(txr_ref[at, :], (rest, LANES)), halo - radius, 1, stride=1, stride_axis=0)
        at_row = row * height + rest_begin - halo + lane
        inside = (at_row >= 0) & (at_row < rows_n * height)
        long = long / jnp.sum(jnp.where(inside, long, 0.0), axis=1, keepdims=True)
        high = long.astype(BF16).astype(F32)
        zero = jnp.zeros(long.shape, F32)
        first = jnp.concatenate([high, zero], axis=1)
        second = jnp.concatenate([long - high, zero], axis=1)
        ar[z] = (first + pltpu.roll(second, rk, 1) + pltpu.roll(first, 2 * rk, 1)).astype(BF16)
        return carry

    def blur_rows(a, v):
        high, low = split(v)
        return jnp.dot(a[:, :3 * kk], jnp.concatenate([high, high, low], axis=0), preferred_element_type=F32)

    def blur_columns(v, w):
        n = v.shape[0]
        parts = [v[:, b * LANES:(b + 1) * LANES] for b in blocks]
        wide = []
        for b in blocks:
            outer = jnp.zeros((n, LANES), F32)
            if b > 0:
                outer = jnp.where(lane < 2 * halo, pltpu.roll(parts[b - 1], 2 * halo, 1), outer)
            outer = jnp.where(lane < halo, parts[b + 1] if b < blocks[-1] else 0.0, outer)
            wide.append(jnp.concatenate([parts[b], outer], axis=1))
        wide = jnp.concatenate(split(jnp.concatenate(wide, axis=0)), axis=0)
        both = jnp.dot(wide[:, :LANES + 2 * halo], w, preferred_element_type=F32)
        m = n * len(blocks)
        made = both[:m, :LANES] + both[m:, :LANES] + both[:m, LANES:]
        return jnp.concatenate([made[b * n:(b + 1) * n] for b in blocks], axis=1)

    def edge(it, which, p):
        if p in (0, chunks - 1):
            x_recv(it, which, p)

    def planes(make, put, group=GROUP):
        def body(n, carry):
            made = [make(n * group + i) for i in range(group)]
            for i, v in enumerate(made):
                put(n * group + i, v)
            return carry
        lax.fori_loop(0, depth // group, body, 0, unroll=PASSES)

    def stage_xy(it, p):
        edge(it, 0, p)
        c = begin(p)

        def make(z):
            return blur_columns(blur_rows(af[z], ext[it, z, pl.ds(c, kk), :]), wf[z])

        def put(z, v):
            bz[it, radius + z, pl.ds(c, CHUNK), :] = v
        planes(make, put)
        z_start(it, 0, p)

    def blur_depth(buf, it, tile, lanes, flip):
        total = None
        for k in range(taps):
            weight = tz_ref[taps - 1 - k] if flip else tz_ref[k]
            term = weight * buf[it, k:k + depth, tile, lanes]
            total = term if total is None else total + term
        return total

    def tiles(p):
        for r in range(0, CHUNK, 8):
            for l in range(0, width, LANES):
                yield pl.ds(begin(p, r, 8), 8), pl.ds(begin(p, halo + r, 8), 8), slice(l, l + LANES)

    def stage_ratio(it, p):
        for tile, inner, lanes in tiles(p):
            blurred = blur_depth(bz, it, tile, lanes, False)
            rz[it, radius:radius + depth, tile, lanes] = ext[0, :, inner, lanes] / blurred
        z_start(it, 1, p)

    def stage_zy(it, p):
        for r in range(0, CHUNK, 8):
            for l in range(0, width, LANES):
                lanes = slice(l, l + LANES)
                mid[:, r:r + 8, lanes] = blur_depth(rz, it, pl.ds(begin(p, r, 8), 8), lanes, True)
        rows = pl.ds(begin(p, halo), CHUNK)

        def put(z, v):
            dext[it, z, rows, :] = v
        planes(lambda z: blur_columns(mid[z], wa[z]) * scale[z], put)
        if p in (0, chunks - 1):
            x_start(it, 1, p)

    def stage_x(it, p):
        edge(it, 1, p)
        c = begin(p)
        inner = pl.ds(begin(p, halo), CHUNK)

        def make(z):
            return ext[it, z, inner, :] * blur_rows(aa[z, chunk(p)], dext[it, z, pl.ds(c, kk), :])

        def put(z, v):
            if it == ITERS - 1:
                out_ref[z, pl.ds(c, CHUNK), :] = v
            else:
                ext[it + 1, z, inner, :] = v
        planes(make, put)
        if it < ITERS - 1 and p in (0, chunks - 1):
            x_start(it + 1, 0, p)

    def stage_rest():
        edge(ITERS - 1, 1, chunks - 1)

        def make(z):
            high, low = split(dext[ITERS - 1, z, pl.ds(rest_begin, rk), :])
            v = jnp.dot(ar[z][:, :3 * rk], jnp.concatenate([high, high, low], axis=0), preferred_element_type=F32)
            return ext[ITERS - 1, z, pl.ds(pl.multiple_of(rest_begin + halo, CHUNK), rest), :] * v

        def put(z, v):
            out_ref[z, pl.ds(rest_begin, rest), :] = v
        planes(make, put, 4)

    clear("row", ext, 0)
    lax.fori_loop(0, depth, build_forward, 0, unroll=4)
    pl.semaphore_wait(barrier, sum(there.astype(jnp.int32) for there, _ in sides.values()))
    fetches[0].wait()
    for p in (0, chunks - 1):
        x_start(0, 0, p)
    started = 0
    for it in range(ITERS):
        order = chunk_order(chunks, it)
        for p in order[started:]:
            stage_xy(it, p)
        if it == 0:
            lax.fori_loop(0, depth, build_adjoint, 0)
            for buffer in (bz, rz):
                for i in range(ITERS):
                    clear("slab", buffer, i)
            for i in range(ITERS):
                clear("row", dext, i)
            for i in range(1, ITERS):
                clear("row", ext, i)
        for p in order:
            z_recv(it, 0, p)
            stage_ratio(it, p)
        ready = list(range(chunks - 2)) if it < ITERS - 1 else []
        for n, p in enumerate(order[:-1]):
            z_recv(it, 1, p)
            stage_zy(it, p)
            have = order[:n + 1]
            for q in [q for q in ready if all(o in have for o in (q - 1, q, q + 1) if 0 <= o < chunks)]:
                ready.remove(q)
                stage_x(it, q)
        if it < ITERS - 1:
            for p in range(chunks - 3):
                stage_xy(it + 1, p)
            z_recv(it, 1, order[-1])
            stage_zy(it, order[-1])
            stage_x(it, chunks - 2)
            stage_xy(it + 1, chunks - 3)
            stage_x(it, chunks - 1)
            started = chunks - 2
        else:
            early = [p for p in range(chunks) if abs(p - order[-1]) > 1]
            for p in early:
                stage_x(it, p)
            z_recv(it, 1, order[-1])
            stage_zy(it, order[-1])
            if early == [0] and 3 * rk <= 2 * LANES:
                stage_rest()
            else:
                for p in range(chunks):
                    if p not in early:
                        stage_x(it, p)

    for axis, side, make in sends:
        sent(axis, side, make)


def solution(mesh):
    rows_n, slabs_n = mesh.shape["row"], mesh.shape["slab"]

    def on_device(observed, band_index, taps_x, taps_y, taps_z):
        depth, height, width = observed.shape
        bands, taps = taps_x.shape
        radius = taps // 2

        vmem = pl.BlockSpec(memory_space=pltpu.VMEM)
        hbm = pl.BlockSpec(memory_space=pltpu.HBM)
        chunks = height // CHUNK
        return pl.pallas_call(
            functools.partial(kernel, rows_n, slabs_n, taps),
            out_shape=jax.ShapeDtypeStruct(observed.shape, F32),
            in_specs=[hbm] * 5,
            out_specs=vmem,
            scratch_shapes=[
                pltpu.SMEM((depth,), jnp.int32),
                pltpu.SMEM((taps,), F32),
                pltpu.VMEM((bands, taps), F32),
                pltpu.VMEM((bands, taps), F32),
                pltpu.SemaphoreType.DMA((5,)),
            ] + [pltpu.VMEM((bands, LANES), F32)] * 4 + [
                pltpu.VMEM((ITERS, depth, height + 2 * CHUNK, width), F32),
                pltpu.VMEM((ITERS, depth, height + 2 * CHUNK, width), F32),
                pltpu.VMEM((ITERS, depth + 2 * radius, height, width), F32),
                pltpu.VMEM((ITERS, depth + 2 * radius, height, width), F32),
                pltpu.VMEM((depth, LANES + 2 * CHUNK, 2 * LANES), BF16),
                pltpu.VMEM((depth, LANES + 2 * CHUNK, 2 * LANES), BF16),
                pltpu.VMEM((depth, 1, width), F32),
                pltpu.VMEM((depth, CHUNK, 2 * LANES), BF16),
                pltpu.VMEM((depth, chunks, CHUNK, 2 * LANES), BF16),
                pltpu.VMEM((depth, height - CHUNK, 2 * LANES), BF16),
                pltpu.VMEM((depth, CHUNK, width), F32),
                pltpu.SemaphoreType.DMA((ITERS, 2, chunks, 2)),
                pltpu.SemaphoreType.DMA((ITERS, 2, chunks, 2)),
                pltpu.SemaphoreType.DMA((ITERS, 2, 2)),
                pltpu.SemaphoreType.DMA((ITERS, 2, 2)),
            ],
            compiler_params=pltpu.CompilerParams(
                collective_id=0, has_side_effects=True, vmem_limit_bytes=48 * 1024 * 1024
            ),
        )(
            *[pltpu.with_memory_space_constraint(v, pltpu.HBM) for v in (band_index, taps_z, taps_x, taps_y, observed)]
        )

    in_specs = (P(("grp", "slab"), "row", None), P("slab"), P(), P(), P())
    return jax.shard_map(
        on_device, mesh=mesh, in_specs=in_specs, out_specs=P(("grp", "slab"), "row", None), check_vma=False
    )
```

```python
import functools

import jax
import jax.numpy as jnp
from jax import lax
from jax.experimental import pallas as pl
from jax.experimental.pallas import tpu as pltpu
from jax.sharding import PartitionSpec as P

ITERS = 2
CHUNK = 16
LANES = 128
GROUP = 8
PASSES = 1
F32 = jnp.float32
BF16 = jnp.bfloat16


def split(v):
    high = v.astype(BF16)
    return high, (v - high.astype(F32)).astype(BF16)


def chunk_order(count, it):
    first = [1, 0] if it == 0 else [0, 1]
    inner = list(range(2, count - 1))
    return first + ([count - 1] + inner if it == ITERS - 1 else inner + [count - 1])


def kernel(
    rows_n, slabs_n, taps,
    band_hbm, tz_hbm, tx_hbm, ty_hbm, obs_hbm,
    out_ref,
    band_ref, tz_ref, tx_ref, ty_ref, in_sem,
    txf_ref, txr_ref, tyf_ref, tyr_ref, ext, dext, bz, rz, wf, wa, scale, af, aa, ar, mid,
    zs_sem, zr_sem, xs_sem, xr_sem,
):
    depth, height, width = obs_hbm.shape
    radius = taps // 2
    halo = CHUNK
    chunks = height // CHUNK
    row = lax.axis_index("row")
    slab = lax.axis_index("slab")
    parity = row % 2

    def chunk(p):
        return p + parity * (chunks - 1 - 2 * p)

    def begin(p, more=0, unit=CHUNK):
        return pl.multiple_of(chunk(p) * CHUNK + more, unit)

    fetches = [
        pltpu.make_async_copy(src, dst, in_sem.at[n])
        for n, (src, dst) in enumerate((
            (obs_hbm, ext.at[0, :, pl.ds(halo, height), :]),
            (ty_hbm, ty_ref), (tx_hbm, tx_ref), (band_hbm, band_ref), (tz_hbm, tz_ref),
        ))
    ]
    for fetch in fetches:
        fetch.start()

    sides = {
        ("row", 0): (row < rows_n - 1, row + 1),
        ("row", 1): (row > 0, row - 1),
        ("slab", 0): (slab < slabs_n - 1, slab + 1),
        ("slab", 1): (slab > 0, slab - 1),
    }

    barrier = pltpu.get_barrier_semaphore()
    for (axis, _), (there, index) in sides.items():
        @pl.when(there)
        def _(axis=axis, index=index):
            pl.semaphore_signal(barrier, inc=1, device_id={axis: index}, device_id_type=pl.DeviceIdType.MESH)

    def clear(axis, buffer, it):
        for side in range(2):
            @pl.when(jnp.logical_not(sides[(axis, side)][0]))
            def _():
                if axis == "row":
                    first = 0 if side == 1 else halo + height
                    buffer[it, :, first:first + halo, :] = jnp.zeros((depth, halo, width), F32)
                else:
                    first = 0 if side == 1 else radius + depth
                    buffer[it, first:first + radius] = jnp.zeros((radius, height, width), F32)

    def row_copy(src, dst, it, which, side):
        if side == 0:
            src_start, dst_start = src[1] + height - halo, 0
        else:
            src_start, dst_start = src[1], halo + height
        return pltpu.make_async_remote_copy(
            src_ref=src[0].at[:, pl.ds(src_start, halo), :],
            dst_ref=dst.at[it, :, pl.ds(dst_start, halo), :],
            send_sem=xs_sem.at[it, which, side],
            recv_sem=xr_sem.at[it, which, side],
            device_id={"row": sides[("row", side)][1]},
            device_id_type=pl.DeviceIdType.MESH,
        )

    def slab_copy(buf, it, which, c, side):
        if side == 0:
            src_start, dst_start = depth, 0
        else:
            src_start, dst_start = radius, radius + depth
        span = pl.ds(begin(c), CHUNK)
        return pltpu.make_async_remote_copy(
            src_ref=buf.at[it, pl.ds(src_start, radius), span, :],
            dst_ref=buf.at[it, pl.ds(dst_start, radius), span, :],
            send_sem=zs_sem.at[it, which, c, side],
            recv_sem=zr_sem.at[it, which, c, side],
            device_id={"slab": sides[("slab", side)][1]},
            device_id_type=pl.DeviceIdType.MESH,
        )

    def start(axis, side, make, also=True):
        @pl.when(sides[(axis, side)][0] & also)
        def _():
            make(side).start()

    def recv(axis, side, make, also=True):
        @pl.when(sides[(axis, 1 - side)][0] & also)
        def _():
            make(side).wait_recv()

    def sent(axis, side, make):
        @pl.when(sides[(axis, side)][0])
        def _():
            make(side).wait_send()

    sends = []

    def x_make(it, which):
        buffer = ext if which == 0 else dext
        return functools.partial(row_copy, (buffer.at[it], halo), buffer, it, which)

    def z_make(it, which, c):
        return functools.partial(slab_copy, bz if which == 0 else rz, it, which, c)

    def x_start(it, which, p):
        near = p == 0
        for v in range(2):
            side = 1 - v if near else v
            start("row", side, x_make(it, which), parity == v)
        if near:
            sends.extend(("row", side, x_make(it, which)) for side in range(2))

    def x_recv(it, which, p):
        near = p == 0
        for v in range(2):
            recv("row", v if near else 1 - v, x_make(it, which), parity == v)

    def z_start(it, which, c):
        for side in range(2):
            start("slab", side, z_make(it, which, c))
            sends.append(("slab", side, z_make(it, which, c)))

    def z_recv(it, which, c):
        for side in range(2):
            recv("slab", side, z_make(it, which, c))

    for fetch in fetches[1:]:
        fetch.wait()

    kk = 3 * halo
    rest = height - CHUNK
    rest_begin = pl.multiple_of((1 - parity) * CHUNK, CHUNK)
    rk = rest + 2 * halo
    mirror = (
        lax.broadcasted_iota(jnp.int32, (LANES, LANES), 0) + lax.broadcasted_iota(jnp.int32, (LANES, LANES), 1)
        == taps - 1
    ).astype(F32)
    for source, ahead in ((tx_ref, txf_ref), (ty_ref, tyf_ref)):
        ahead[...] = jnp.zeros(ahead.shape, F32)
        ahead[:, 0:taps] = source[...]

    def turn(ahead, back):
        back[...] = jnp.dot(ahead[...], mirror, precision=lax.Precision.HIGHEST, preferred_element_type=F32)
    turn(tyf_ref, tyr_ref)

    lane = lax.broadcasted_iota(jnp.int32, (1, LANES), 1)
    blocks = range(width // LANES)

    def column_band(line):
        gap = lax.broadcasted_iota(jnp.int32, (LANES, LANES), 0) - lane
        ring = pltpu.roll(jnp.broadcast_to(line, (LANES, LANES)), LANES - radius, 1, stride=1, stride_axis=0)
        main = jnp.where((gap <= radius) & (gap >= -radius), ring, 0.0)
        short = jnp.broadcast_to(line, (halo, LANES))
        after = pltpu.roll(short, LANES - radius, 1, stride=1, stride_axis=0)
        after = jnp.where(lane >= LANES - radius, after, 0.0)
        before = pltpu.roll(short, LANES - halo - radius, 1, stride=1, stride_axis=0)
        before = jnp.where(lane < radius, before, 0.0)
        return main, after, before

    def store_band(w, z, band):
        for start, part in zip((0, LANES, LANES + halo), band):
            high, low = split(part)
            w[z, start:start + part.shape[0], 0:LANES] = high
            w[z, start:start + part.shape[0], LANES:2 * LANES] = low

    def store_rows(a):
        high = a.astype(BF16).astype(F32)
        low = a - high
        zero = jnp.zeros(a.shape, F32)
        first = jnp.concatenate([high, zero], axis=1)
        second = jnp.concatenate([low, zero], axis=1)
        return (first + pltpu.roll(second, kk, 1) + pltpu.roll(first, 2 * kk, 1)).astype(BF16)

    def row_band(line):
        return pltpu.roll(jnp.broadcast_to(line, (CHUNK, LANES)), halo - radius, 1, stride=1, stride_axis=0)

    def build_forward(z, carry):
        at = pl.ds(band_ref[z], 1)
        store_band(wf, z, column_band(tyr_ref[at, :]))
        af[z] = store_rows(row_band(txf_ref[at, :]))
        return carry

    def build_adjoint(z, carry):
        at = pl.ds(band_ref[z], 1)
        band = column_band(tyf_ref[at, :])
        store_band(wa, z, band)
        tzv = jnp.zeros((1, LANES), F32)
        for k in range(taps):
            tzv = jnp.where(lane == k, tz_ref[k], tzv)
        plane = slab * depth + z + radius - lane
        inside = (plane >= 0) & (plane < slabs_n * depth)
        cz = jnp.sum(jnp.where(inside, tzv, 0.0), axis=1, keepdims=True)
        main, after, before = [jnp.sum(part, axis=0, keepdims=True) for part in band]
        for j in blocks:
            total = main
            if j > 0:
                total = total + before
            if j < blocks[-1]:
                total = total + after
            scale[z, :, j * LANES:(j + 1) * LANES] = 1.0 / (total * cz)
        base = row_band(txr_ref[at, :])
        for c in range(chunks):
            at_row = row * height + (c - 1) * CHUNK + lax.broadcasted_iota(jnp.int32, (CHUNK, LANES), 1)
            inside = (at_row >= 0) & (at_row < rows_n * height)
            aa[z, c] = store_rows(base / jnp.sum(jnp.where(inside, base, 0.0), axis=1, keepdims=True))
        long = pltpu.roll(
            jnp.broadcast_to(txr_ref[at, :], (rest, LANES)), halo - radius, 1, stride=1, stride_axis=0)
        at_row = row * height + rest_begin - halo + lane
        inside = (at_row >= 0) & (at_row < rows_n * height)
        long = long / jnp.sum(jnp.where(inside, long, 0.0), axis=1, keepdims=True)
        high = long.astype(BF16).astype(F32)
        zero = jnp.zeros(long.shape, F32)
        first = jnp.concatenate([high, zero], axis=1)
        second = jnp.concatenate([long - high, zero], axis=1)
        ar[z] = (first + pltpu.roll(second, rk, 1) + pltpu.roll(first, 2 * rk, 1)).astype(BF16)
        return carry

    def blur_rows(a, v):
        high, low = split(v)
        return jnp.dot(a[:, :3 * kk], jnp.concatenate([high, high, low], axis=0), preferred_element_type=F32)

    def blur_columns(v, w):
        n = v.shape[0]
        parts = [v[:, b * LANES:(b + 1) * LANES] for b in blocks]
        wide = []
        for b in blocks:
            outer = pltpu.roll(parts[b - 1], 2 * halo, 1) if b > 0 else 0.0
            outer = jnp.where(lane < halo, parts[b + 1] if b < blocks[-1] else 0.0, outer)
            wide.append(jnp.concatenate([parts[b], outer], axis=1))
        wide = jnp.concatenate(split(jnp.concatenate(wide, axis=0)), axis=0)
        both = jnp.dot(wide[:, :LANES + 2 * halo], w, preferred_element_type=F32)
        m = n * len(blocks)
        made = both[:m, :LANES] + both[m:, :LANES] + both[:m, LANES:]
        return jnp.concatenate([made[b * n:(b + 1) * n] for b in blocks], axis=1)

    def edge(it, which, p):
        if p in (0, chunks - 1):
            x_recv(it, which, p)

    def planes(make, put, group=GROUP, finish=None, part=None):
        def body(n, carry):
            made = [make(n * group + i) for i in range(group)]
            if finish is not None:
                made = [finish(n * group + i, v) for i, v in enumerate(made)]
            for i, v in enumerate(made):
                put(n * group + i, v)
            return carry
        lax.fori_loop(0, depth // group, body, 0, unroll=PASSES)

    def stage_xy(it, p):
        edge(it, 0, p)
        c = begin(p)

        def make(z):
            return blur_rows(af[z], ext[it, z, pl.ds(c, kk), :])

        def finish(z, v):
            return blur_columns(v, wf[z])

        def put(z, v):
            bz[it, radius + z, pl.ds(c, CHUNK), :] = v
        planes(make, put, GROUP, finish)
        z_start(it, 0, p)

    def blur_depth(buf, it, tile, lanes, flip):
        total = None
        for k in range(taps):
            weight = tz_ref[taps - 1 - k] if flip else tz_ref[k]
            term = weight * buf[it, k:k + depth, tile, lanes]
            total = term if total is None else total + term
        return total

    def tiles(p):
        for r in range(0, CHUNK, 8):
            for l in range(0, width, LANES):
                yield pl.ds(begin(p, r, 8), 8), pl.ds(begin(p, halo + r, 8), 8), slice(l, l + LANES)

    def stage_ratio(it, p):
        for tile, inner, lanes in tiles(p):
            blurred = blur_depth(bz, it, tile, lanes, False)
            rz[it, radius:radius + depth, tile, lanes] = ext[0, :, inner, lanes] / blurred
        z_start(it, 1, p)

    def stage_zy(it, p):
        for r in range(0, CHUNK, 8):
            for l in range(0, width, LANES):
                lanes = slice(l, l + LANES)
                mid[:, r:r + 8, lanes] = blur_depth(rz, it, pl.ds(begin(p, r, 8), 8), lanes, True)
        rows = pl.ds(begin(p, halo), CHUNK)

        def put(z, v):
            dext[it, z, rows, :] = v
        planes(lambda z: blur_columns(mid[z], wa[z]) * scale[z], put)
        if p in (0, chunks - 1):
            x_start(it, 1, p)

    def stage_x(it, p):
        edge(it, 1, p)
        c = begin(p)
        inner = pl.ds(begin(p, halo), CHUNK)

        def make(z):
            return ext[it, z, inner, :] * blur_rows(aa[z, chunk(p)], dext[it, z, pl.ds(c, kk), :])

        def put(z, v):
            if it == ITERS - 1:
                out_ref[z, pl.ds(c, CHUNK), :] = v
            else:
                ext[it + 1, z, inner, :] = v
        planes(make, put)
        if it < ITERS - 1 and p in (0, chunks - 1):
            x_start(it + 1, 0, p)

    def stage_rest():
        edge(ITERS - 1, 1, chunks - 1)

        def make(z):
            high, low = split(dext[ITERS - 1, z, pl.ds(rest_begin, rk), :])
            v = jnp.dot(ar[z][:, :3 * rk], jnp.concatenate([high, high, low], axis=0), preferred_element_type=F32)
            return ext[ITERS - 1, z, pl.ds(pl.multiple_of(rest_begin + halo, CHUNK), rest), :] * v

        def put(z, v):
            out_ref[z, pl.ds(rest_begin, rest), :] = v
        planes(make, put, 4)

    clear("row", ext, 0)
    lax.fori_loop(0, depth, build_forward, 0, unroll=4)
    pl.semaphore_wait(barrier, sum(there.astype(jnp.int32) for there, _ in sides.values()))
    fetches[0].wait()
    for p in (0, chunks - 1):
        x_start(0, 0, p)
    started = 0
    for it in range(ITERS):
        order = chunk_order(chunks, it)
        for p in order[started:]:
            stage_xy(it, p)
        if it == 0:
            turn(txf_ref, txr_ref)
            lax.fori_loop(0, depth, build_adjoint, 0)
            for buffer in (bz, rz):
                for i in range(ITERS):
                    clear("slab", buffer, i)
            for i in range(ITERS):
                clear("row", dext, i)
            for i in range(1, ITERS):
                clear("row", ext, i)
        for p in order:
            z_recv(it, 0, p)
            stage_ratio(it, p)
        ready = list(range(chunks - 2)) if it < ITERS - 1 else []
        for n, p in enumerate(order[:-1]):
            z_recv(it, 1, p)
            stage_zy(it, p)
            have = order[:n + 1]
            for q in [q for q in ready if all(o in have for o in (q - 1, q, q + 1) if 0 <= o < chunks)]:
                ready.remove(q)
                stage_x(it, q)
        if it < ITERS - 1:
            for p in range(chunks - 3):
                stage_xy(it + 1, p)
            z_recv(it, 1, order[-1])
            stage_zy(it, order[-1])
            stage_x(it, chunks - 2)
            stage_xy(it + 1, chunks - 3)
            stage_x(it, chunks - 1)
            started = chunks - 2
        else:
            early = [p for p in range(chunks) if abs(p - order[-1]) > 1]
            for p in early:
                stage_x(it, p)
            z_recv(it, 1, order[-1])
            stage_zy(it, order[-1])
            if early == [0] and 3 * rk <= 2 * LANES:
                stage_rest()
            else:
                for p in range(chunks):
                    if p not in early:
                        stage_x(it, p)

    for axis, side, make in sends:
        sent(axis, side, make)


def solution(mesh):
    rows_n, slabs_n = mesh.shape["row"], mesh.shape["slab"]

    def on_device(observed, band_index, taps_x, taps_y, taps_z):
        depth, height, width = observed.shape
        bands, taps = taps_x.shape
        radius = taps // 2

        vmem = pl.BlockSpec(memory_space=pltpu.VMEM)
        hbm = pl.BlockSpec(memory_space=pltpu.HBM)
        chunks = height // CHUNK
        return pl.pallas_call(
            functools.partial(kernel, rows_n, slabs_n, taps),
            out_shape=jax.ShapeDtypeStruct(observed.shape, F32),
            in_specs=[hbm] * 5,
            out_specs=vmem,
            scratch_shapes=[
                pltpu.SMEM((depth,), jnp.int32),
                pltpu.SMEM((taps,), F32),
                pltpu.VMEM((bands, taps), F32),
                pltpu.VMEM((bands, taps), F32),
                pltpu.SemaphoreType.DMA((5,)),
            ] + [pltpu.VMEM((bands, LANES), F32)] * 4 + [
                pltpu.VMEM((ITERS, depth, height + 2 * CHUNK, width), F32),
                pltpu.VMEM((ITERS, depth, height + 2 * CHUNK, width), F32),
                pltpu.VMEM((ITERS, depth + 2 * radius, height, width), F32),
                pltpu.VMEM((ITERS, depth + 2 * radius, height, width), F32),
                pltpu.VMEM((depth, LANES + 2 * CHUNK, 2 * LANES), BF16),
                pltpu.VMEM((depth, LANES + 2 * CHUNK, 2 * LANES), BF16),
                pltpu.VMEM((depth, 1, width), F32),
                pltpu.VMEM((depth, CHUNK, 2 * LANES), BF16),
                pltpu.VMEM((depth, chunks, CHUNK, 2 * LANES), BF16),
                pltpu.VMEM((depth, height - CHUNK, 2 * LANES), BF16),
                pltpu.VMEM((depth, CHUNK, width), F32),
                pltpu.SemaphoreType.DMA((ITERS, 2, chunks, 2)),
                pltpu.SemaphoreType.DMA((ITERS, 2, chunks, 2)),
                pltpu.SemaphoreType.DMA((ITERS, 2, 2)),
                pltpu.SemaphoreType.DMA((ITERS, 2, 2)),
            ],
            compiler_params=pltpu.CompilerParams(
                collective_id=0, has_side_effects=True, vmem_limit_bytes=48 * 1024 * 1024
            ),
        )(
            *[pltpu.with_memory_space_constraint(v, pltpu.HBM) for v in (band_index, taps_z, taps_x, taps_y, observed)]
        )

    in_specs = (P(("grp", "slab"), "row", None), P("slab"), P(), P(), P())
    return jax.shard_map(
        on_device, mesh=mesh, in_specs=in_specs, out_specs=P(("grp", "slab"), "row", None), check_vma=False
    )
```

```python
import functools

import jax
import jax.numpy as jnp
from jax import lax
from jax.experimental import pallas as pl
from jax.experimental.pallas import tpu as pltpu
from jax.sharding import PartitionSpec as P

ITERS = 2
CHUNK = 16
LANES = 128
GROUP = 8
PASSES = 1
F32 = jnp.float32
BF16 = jnp.bfloat16


def split(v):
    high = v.astype(BF16)
    return high, (v - high.astype(F32)).astype(BF16)


def chunk_order(count, it):
    first = [1, 0] if it == 0 else [0, 1]
    inner = list(range(2, count - 1))
    return first + ([count - 1] + inner if it == ITERS - 1 else inner + [count - 1])


def kernel(
    rows_n, slabs_n, taps,
    band_hbm, tz_hbm, tx_hbm, ty_hbm, obs_hbm,
    out_ref,
    band_ref, tz_ref, tx_ref, ty_ref, in_sem,
    txf_ref, txr_ref, tyf_ref, tyr_ref, ext, dext, bz, rz, wf, wa, scale, af, aa, ar, mid,
    zs_sem, zr_sem, xs_sem, xr_sem,
):
    depth, height, width = obs_hbm.shape
    radius = taps // 2
    halo = CHUNK
    chunks = height // CHUNK
    row = lax.axis_index("row")
    slab = lax.axis_index("slab")
    parity = row % 2

    def chunk(p):
        return p + parity * (chunks - 1 - 2 * p)

    def begin(p, more=0, unit=CHUNK):
        return pl.multiple_of(chunk(p) * CHUNK + more, unit)

    fetches = [
        pltpu.make_async_copy(src, dst, in_sem.at[n])
        for n, (src, dst) in enumerate((
            (obs_hbm, ext.at[0, :, pl.ds(halo, height), :]),
            (ty_hbm, ty_ref), (tx_hbm, tx_ref), (band_hbm, band_ref), (tz_hbm, tz_ref),
        ))
    ]
    for fetch in fetches:
        fetch.start()

    sides = {
        ("row", 0): (row < rows_n - 1, row + 1),
        ("row", 1): (row > 0, row - 1),
        ("slab", 0): (slab < slabs_n - 1, slab + 1),
        ("slab", 1): (slab > 0, slab - 1),
    }

    barrier = pltpu.get_barrier_semaphore()
    for (axis, _), (there, index) in sides.items():
        @pl.when(there)
        def _(axis=axis, index=index):
            pl.semaphore_signal(barrier, inc=1, device_id={axis: index}, device_id_type=pl.DeviceIdType.MESH)

    def clear(axis, buffer, it):
        for side in range(2):
            @pl.when(jnp.logical_not(sides[(axis, side)][0]))
            def _():
                if axis == "row":
                    first = 0 if side == 1 else halo + height
                    buffer[it, :, first:first + halo, :] = jnp.zeros((depth, halo, width), F32)
                else:
                    first = 0 if side == 1 else radius + depth
                    buffer[it, first:first + radius] = jnp.zeros((radius, height, width), F32)

    def row_copy(src, dst, it, which, side):
        if side == 0:
            src_start, dst_start = src[1] + height - halo, 0
        else:
            src_start, dst_start = src[1], halo + height
        return pltpu.make_async_remote_copy(
            src_ref=src[0].at[:, pl.ds(src_start, halo), :],
            dst_ref=dst.at[it, :, pl.ds(dst_start, halo), :],
            send_sem=xs_sem.at[it, which, side],
            recv_sem=xr_sem.at[it, which, side],
            device_id={"row": sides[("row", side)][1]},
            device_id_type=pl.DeviceIdType.MESH,
        )

    def planes_of(side, n):
        first, end = (depth - radius, depth) if side == 0 else (0, radius)
        first, end = max(first, n * GROUP), min(end, (n + 1) * GROUP)
        return first, end - first

    pieces = (
        [[planes_of(side, n) + (0, CHUNK) for side in range(2)] for n in range(depth // GROUP)],
        [[(first, radius, r, 8) for first in (depth - radius, 0)] for r in range(0, CHUNK, 8)],
    )

    def slab_copy(buf, it, which, c, piece, side):
        first, count, r, rows = pieces[which][piece][side]
        moved = -depth if side == 0 else depth
        span = pl.ds(begin(c, r, 8), rows)
        return pltpu.make_async_remote_copy(
            src_ref=buf.at[it, pl.ds(radius + first, count), span, :],
            dst_ref=buf.at[it, pl.ds(radius + first + moved, count), span, :],
            send_sem=zs_sem.at[it, which, c, piece, side],
            recv_sem=zr_sem.at[it, which, c, piece, side],
            device_id={"slab": sides[("slab", side)][1]},
            device_id_type=pl.DeviceIdType.MESH,
        )

    def start(axis, side, make, also=True):
        @pl.when(sides[(axis, side)][0] & also)
        def _():
            make(side).start()

    def recv(axis, side, make, also=True):
        @pl.when(sides[(axis, 1 - side)][0] & also)
        def _():
            make(side).wait_recv()

    def sent(axis, side, make):
        @pl.when(sides[(axis, side)][0])
        def _():
            make(side).wait_send()

    sends = []

    def x_make(it, which):
        buffer = ext if which == 0 else dext
        return functools.partial(row_copy, (buffer.at[it], halo), buffer, it, which)

    def z_make(it, which, c, piece):
        return functools.partial(slab_copy, bz if which == 0 else rz, it, which, c, piece)

    def x_start(it, which, p):
        near = p == 0
        for v in range(2):
            side = 1 - v if near else v
            start("row", side, x_make(it, which), parity == v)
        if near:
            sends.extend(("row", side, x_make(it, which)) for side in range(2))

    def x_recv(it, which, p):
        near = p == 0
        for v in range(2):
            recv("row", v if near else 1 - v, x_make(it, which), parity == v)

    def z_start(it, which, c, piece):
        for side in range(2):
            start("slab", side, z_make(it, which, c, piece))
            sends.append(("slab", side, z_make(it, which, c, piece)))

    def z_recv(it, which, c, only=None):
        for piece in range(len(pieces[which])) if only is None else [only]:
            for side in range(2):
                recv("slab", side, z_make(it, which, c, piece))

    for fetch in fetches[1:]:
        fetch.wait()

    kk = 3 * halo
    rest = height - CHUNK
    rest_begin = pl.multiple_of((1 - parity) * CHUNK, CHUNK)
    rk = rest + 2 * halo
    mirror = (
        lax.broadcasted_iota(jnp.int32, (LANES, LANES), 0) + lax.broadcasted_iota(jnp.int32, (LANES, LANES), 1)
        == taps - 1
    ).astype(F32)
    for source, ahead in ((tx_ref, txf_ref), (ty_ref, tyf_ref)):
        ahead[...] = jnp.zeros(ahead.shape, F32)
        ahead[:, 0:taps] = source[...]

    def turn(ahead, back):
        back[...] = jnp.dot(ahead[...], mirror, precision=lax.Precision.HIGHEST, preferred_element_type=F32)
    turn(tyf_ref, tyr_ref)

    lane = lax.broadcasted_iota(jnp.int32, (1, LANES), 1)
    blocks = range(width // LANES)

    def column_band(line):
        gap = lax.broadcasted_iota(jnp.int32, (LANES, LANES), 0) - lane
        ring = pltpu.roll(jnp.broadcast_to(line, (LANES, LANES)), LANES - radius, 1, stride=1, stride_axis=0)
        main = jnp.where((gap <= radius) & (gap >= -radius), ring, 0.0)
        short = jnp.broadcast_to(line, (halo, LANES))
        after = pltpu.roll(short, LANES - radius, 1, stride=1, stride_axis=0)
        after = jnp.where(lane >= LANES - radius, after, 0.0)
        before = pltpu.roll(short, LANES - halo - radius, 1, stride=1, stride_axis=0)
        before = jnp.where(lane < radius, before, 0.0)
        return main, after, before

    def store_band(w, z, band):
        for start, part in zip((0, LANES, LANES + halo), band):
            high, low = split(part)
            w[z, start:start + part.shape[0], 0:LANES] = high
            w[z, start:start + part.shape[0], LANES:2 * LANES] = low

    def store_rows(a):
        high = a.astype(BF16).astype(F32)
        low = a - high
        zero = jnp.zeros(a.shape, F32)
        first = jnp.concatenate([high, zero], axis=1)
        second = jnp.concatenate([low, zero], axis=1)
        return (first + pltpu.roll(second, kk, 1) + pltpu.roll(first, 2 * kk, 1)).astype(BF16)

    def row_band(line):
        return pltpu.roll(jnp.broadcast_to(line, (CHUNK, LANES)), halo - radius, 1, stride=1, stride_axis=0)

    def build_forward(z, carry):
        at = pl.ds(band_ref[z], 1)
        store_band(wf, z, column_band(tyr_ref[at, :]))
        af[z] = store_rows(row_band(txf_ref[at, :]))
        return carry

    def build_adjoint(z, carry):
        at = pl.ds(band_ref[z], 1)
        band = column_band(tyf_ref[at, :])
        store_band(wa, z, band)
        tzv = jnp.zeros((1, LANES), F32)
        for k in range(taps):
            tzv = jnp.where(lane == k, tz_ref[k], tzv)
        plane = slab * depth + z + radius - lane
        inside = (plane >= 0) & (plane < slabs_n * depth)
        cz = jnp.sum(jnp.where(inside, tzv, 0.0), axis=1, keepdims=True)
        main, after, before = [jnp.sum(part, axis=0, keepdims=True) for part in band]
        for j in blocks:
            total = main
            if j > 0:
                total = total + before
            if j < blocks[-1]:
                total = total + after
            scale[z, :, j * LANES:(j + 1) * LANES] = 1.0 / (total * cz)
        base = row_band(txr_ref[at, :])
        for c in range(chunks):
            at_row = row * height + (c - 1) * CHUNK + lax.broadcasted_iota(jnp.int32, (CHUNK, LANES), 1)
            inside = (at_row >= 0) & (at_row < rows_n * height)
            aa[z, c] = store_rows(base / jnp.sum(jnp.where(inside, base, 0.0), axis=1, keepdims=True))
        long = pltpu.roll(
            jnp.broadcast_to(txr_ref[at, :], (rest, LANES)), halo - radius, 1, stride=1, stride_axis=0)
        at_row = row * height + rest_begin - halo + lane
        inside = (at_row >= 0) & (at_row < rows_n * height)
        long = long / jnp.sum(jnp.where(inside, long, 0.0), axis=1, keepdims=True)
        high = long.astype(BF16).astype(F32)
        zero = jnp.zeros(long.shape, F32)
        first = jnp.concatenate([high, zero], axis=1)
        second = jnp.concatenate([long - high, zero], axis=1)
        ar[z] = (first + pltpu.roll(second, rk, 1) + pltpu.roll(first, 2 * rk, 1)).astype(BF16)
        return carry

    def blur_rows(a, v):
        high, low = split(v)
        return jnp.dot(a[:, :3 * kk], jnp.concatenate([high, high, low], axis=0), preferred_element_type=F32)

    def blur_columns(v, w):
        n = v.shape[0]
        parts = [v[:, b * LANES:(b + 1) * LANES] for b in blocks]
        wide = []
        for b in blocks:
            outer = pltpu.roll(parts[b - 1], 2 * halo, 1) if b > 0 else 0.0
            outer = jnp.where(lane < halo, parts[b + 1] if b < blocks[-1] else 0.0, outer)
            wide.append(jnp.concatenate([parts[b], outer], axis=1))
        wide = jnp.concatenate(split(jnp.concatenate(wide, axis=0)), axis=0)
        both = jnp.dot(wide[:, :LANES + 2 * halo], w, preferred_element_type=F32)
        m = n * len(blocks)
        made = both[:m, :LANES] + both[m:, :LANES] + both[:m, LANES:]
        return jnp.concatenate([made[b * n:(b + 1) * n] for b in blocks], axis=1)

    def edge(it, which, p):
        if p in (0, chunks - 1):
            x_recv(it, which, p)

    def planes(make, put, group=GROUP, finish=None, part=None):
        def body(n, carry):
            made = [make(n * group + i) for i in range(group)]
            if finish is not None:
                made = [finish(n * group + i, v) for i, v in enumerate(made)]
            for i, v in enumerate(made):
                put(n * group + i, v)
            return carry
        if part is None:
            lax.fori_loop(0, depth // group, body, 0, unroll=PASSES)
        else:
            body(part, 0)

    def stage_xy(it, p):
        edge(it, 0, p)
        c = begin(p)

        def make(z):
            return blur_rows(af[z], ext[it, z, pl.ds(c, kk), :])

        def finish(z, v):
            return blur_columns(v, wf[z])

        def put(z, v):
            bz[it, radius + z, pl.ds(c, CHUNK), :] = v
        for part in range(len(pieces[0])):
            planes(make, put, GROUP, finish, part)
            z_start(it, 0, p, part)

    def blur_depth(buf, it, tile, lanes, flip):
        total = None
        for k in range(taps):
            weight = tz_ref[taps - 1 - k] if flip else tz_ref[k]
            term = weight * buf[it, k:k + depth, tile, lanes]
            total = term if total is None else total + term
        return total

    def tiles(p):
        for r in range(0, CHUNK, 8):
            for l in range(0, width, LANES):
                yield pl.ds(begin(p, r, 8), 8), pl.ds(begin(p, halo + r, 8), 8), slice(l, l + LANES)

    def stage_ratio(it, p):
        for n, (tile, inner, lanes) in enumerate(tiles(p)):
            blurred = blur_depth(bz, it, tile, lanes, False)
            rz[it, radius:radius + depth, tile, lanes] = ext[0, :, inner, lanes] / blurred
            if (n + 1) % len(blocks) == 0:
                z_start(it, 1, p, n // len(blocks))

    def stage_zy(it, p):
        for r in range(0, CHUNK, 8):
            z_recv(it, 1, p, r // 8)
            for l in range(0, width, LANES):
                lanes = slice(l, l + LANES)
                mid[:, r:r + 8, lanes] = blur_depth(rz, it, pl.ds(begin(p, r, 8), 8), lanes, True)
        rows = pl.ds(begin(p, halo), CHUNK)

        def put(z, v):
            dext[it, z, rows, :] = v
        planes(lambda z: blur_columns(mid[z], wa[z]) * scale[z], put)
        if p in (0, chunks - 1):
            x_start(it, 1, p)

    def stage_x(it, p):
        edge(it, 1, p)
        c = begin(p)
        inner = pl.ds(begin(p, halo), CHUNK)

        def make(z):
            return ext[it, z, inner, :] * blur_rows(aa[z, chunk(p)], dext[it, z, pl.ds(c, kk), :])

        def put(z, v):
            if it == ITERS - 1:
                out_ref[z, pl.ds(c, CHUNK), :] = v
            else:
                ext[it + 1, z, inner, :] = v
        planes(make, put)
        if it < ITERS - 1 and p in (0, chunks - 1):
            x_start(it + 1, 0, p)

    def stage_rest():
        edge(ITERS - 1, 1, chunks - 1)

        def make(z):
            high, low = split(dext[ITERS - 1, z, pl.ds(rest_begin, rk), :])
            v = jnp.dot(ar[z][:, :3 * rk], jnp.concatenate([high, high, low], axis=0), preferred_element_type=F32)
            return ext[ITERS - 1, z, pl.ds(pl.multiple_of(rest_begin + halo, CHUNK), rest), :] * v

        def put(z, v):
            out_ref[z, pl.ds(rest_begin, rest), :] = v
        planes(make, put, 4)

    clear("row", ext, 0)
    lax.fori_loop(0, depth, build_forward, 0, unroll=4)
    pl.semaphore_wait(barrier, sum(there.astype(jnp.int32) for there, _ in sides.values()))
    fetches[0].wait()
    for p in (0, chunks - 1):
        x_start(0, 0, p)
    started = 0
    for it in range(ITERS):
        order = chunk_order(chunks, it)
        for p in order[started:]:
            stage_xy(it, p)
        if it == 0:
            turn(txf_ref, txr_ref)
            lax.fori_loop(0, depth, build_adjoint, 0)
            for buffer in (bz, rz):
                for i in range(ITERS):
                    clear("slab", buffer, i)
            for i in range(ITERS):
                clear("row", dext, i)
            for i in range(1, ITERS):
                clear("row", ext, i)
        for p in order:
            z_recv(it, 0, p)
            stage_ratio(it, p)
        ready = list(range(chunks - 2)) if it < ITERS - 1 else []
        for n, p in enumerate(order[:-1]):
            stage_zy(it, p)
            have = order[:n + 1]
            for q in [q for q in ready if all(o in have for o in (q - 1, q, q + 1) if 0 <= o < chunks)]:
                ready.remove(q)
                stage_x(it, q)
        if it < ITERS - 1:
            for p in range(chunks - 3):
                stage_xy(it + 1, p)
            stage_zy(it, order[-1])
            stage_x(it, chunks - 2)
            stage_xy(it + 1, chunks - 3)
            stage_x(it, chunks - 1)
            started = chunks - 2
        else:
            early = [p for p in range(chunks) if abs(p - order[-1]) > 1]
            for p in early:
                stage_x(it, p)
            stage_zy(it, order[-1])
            if early == [0] and 3 * rk <= 2 * LANES:
                stage_rest()
            else:
                for p in range(chunks):
                    if p not in early:
                        stage_x(it, p)

    for axis, side, make in sends:
        sent(axis, side, make)


def solution(mesh):
    rows_n, slabs_n = mesh.shape["row"], mesh.shape["slab"]

    def on_device(observed, band_index, taps_x, taps_y, taps_z):
        depth, height, width = observed.shape
        bands, taps = taps_x.shape
        radius = taps // 2

        vmem = pl.BlockSpec(memory_space=pltpu.VMEM)
        hbm = pl.BlockSpec(memory_space=pltpu.HBM)
        chunks = height // CHUNK
        return pl.pallas_call(
            functools.partial(kernel, rows_n, slabs_n, taps),
            out_shape=jax.ShapeDtypeStruct(observed.shape, F32),
            in_specs=[hbm] * 5,
            out_specs=vmem,
            scratch_shapes=[
                pltpu.SMEM((depth,), jnp.int32),
                pltpu.SMEM((taps,), F32),
                pltpu.VMEM((bands, taps), F32),
                pltpu.VMEM((bands, taps), F32),
                pltpu.SemaphoreType.DMA((5,)),
            ] + [pltpu.VMEM((bands, LANES), F32)] * 4 + [
                pltpu.VMEM((ITERS, depth, height + 2 * CHUNK, width), F32),
                pltpu.VMEM((ITERS, depth, height + 2 * CHUNK, width), F32),
                pltpu.VMEM((ITERS, depth + 2 * radius, height, width), F32),
                pltpu.VMEM((ITERS, depth + 2 * radius, height, width), F32),
                pltpu.VMEM((depth, LANES + 2 * CHUNK, 2 * LANES), BF16),
                pltpu.VMEM((depth, LANES + 2 * CHUNK, 2 * LANES), BF16),
                pltpu.VMEM((depth, 1, width), F32),
                pltpu.VMEM((depth, CHUNK, 2 * LANES), BF16),
                pltpu.VMEM((depth, chunks, CHUNK, 2 * LANES), BF16),
                pltpu.VMEM((depth, height - CHUNK, 2 * LANES), BF16),
                pltpu.VMEM((depth, CHUNK, width), F32),
                pltpu.SemaphoreType.DMA((ITERS, 2, chunks, max(depth // GROUP, CHUNK // 8), 2)),
                pltpu.SemaphoreType.DMA((ITERS, 2, chunks, max(depth // GROUP, CHUNK // 8), 2)),
                pltpu.SemaphoreType.DMA((ITERS, 2, 2)),
                pltpu.SemaphoreType.DMA((ITERS, 2, 2)),
            ],
            compiler_params=pltpu.CompilerParams(
                collective_id=0, has_side_effects=True, vmem_limit_bytes=48 * 1024 * 1024
            ),
        )(
            *[pltpu.with_memory_space_constraint(v, pltpu.HBM) for v in (band_index, taps_z, taps_x, taps_y, observed)]
        )

    in_specs = (P(("grp", "slab"), "row", None), P("slab"), P(), P(), P())
    return jax.shard_map(
        on_device, mesh=mesh, in_specs=in_specs, out_specs=P(("grp", "slab"), "row", None), check_vma=False
    )
```

```python
import functools

import jax
import jax.numpy as jnp
from jax import lax
from jax.experimental import pallas as pl
from jax.experimental.pallas import tpu as pltpu
from jax.sharding import PartitionSpec as P

ITERS = 2
CHUNK = 16
LANES = 128
GROUP = 8
PASSES = 1
F32 = jnp.float32
BF16 = jnp.bfloat16


def split(v):
    high = v.astype(BF16)
    return high, (v - high.astype(F32)).astype(BF16)


def chunk_order(count, it):
    first = [1, 0] if it == 0 else [0, 1]
    inner = list(range(2, count - 1))
    return first + ([count - 1] + inner if it == ITERS - 1 else inner + [count - 1])


def kernel(
    rows_n, slabs_n, taps,
    band_hbm, tz_hbm, tx_hbm, ty_hbm, obs_hbm,
    out_ref,
    band_ref, tz_ref, tx_ref, ty_ref, in_sem,
    txf_ref, txr_ref, tyf_ref, tyr_ref, ext, dext, bz, rz, wf, wa, scale, af, aa, ar, mid,
    zs_sem, zr_sem, xs_sem, xr_sem,
):
    depth, height, width = obs_hbm.shape
    radius = taps // 2
    halo = CHUNK
    chunks = height // CHUNK
    row = lax.axis_index("row")
    slab = lax.axis_index("slab")
    parity = row % 2

    def chunk(p):
        return p + parity * (chunks - 1 - 2 * p)

    def begin(p, more=0, unit=CHUNK):
        return pl.multiple_of(chunk(p) * CHUNK + more, unit)

    fetches = [
        pltpu.make_async_copy(src, dst, in_sem.at[n])
        for n, (src, dst) in enumerate((
            (obs_hbm, ext.at[0, :, pl.ds(halo, height), :]),
            (ty_hbm, ty_ref), (tx_hbm, tx_ref), (band_hbm, band_ref), (tz_hbm, tz_ref),
        ))
    ]
    for fetch in fetches:
        fetch.start()

    sides = {
        ("row", 0): (row < rows_n - 1, row + 1),
        ("row", 1): (row > 0, row - 1),
        ("slab", 0): (slab < slabs_n - 1, slab + 1),
        ("slab", 1): (slab > 0, slab - 1),
    }

    barrier = pltpu.get_barrier_semaphore()
    for (axis, _), (there, index) in sides.items():
        @pl.when(there)
        def _(axis=axis, index=index):
            pl.semaphore_signal(barrier, inc=1, device_id={axis: index}, device_id_type=pl.DeviceIdType.MESH)

    def clear(axis, buffer, it):
        for side in range(2):
            @pl.when(jnp.logical_not(sides[(axis, side)][0]))
            def _():
                if axis == "row":
                    first = 0 if side == 1 else halo + height
                    buffer[it, :, first:first + halo, :] = jnp.zeros((depth, halo, width), F32)
                else:
                    first = 0 if side == 1 else radius + depth
                    buffer[it, first:first + radius] = jnp.zeros((radius, height, width), F32)

    def row_copy(src, dst, it, which, side):
        if side == 0:
            src_start, dst_start = src[1] + height - halo, 0
        else:
            src_start, dst_start = src[1], halo + height
        return pltpu.make_async_remote_copy(
            src_ref=src[0].at[:, pl.ds(src_start, halo), :],
            dst_ref=dst.at[it, :, pl.ds(dst_start, halo), :],
            send_sem=xs_sem.at[it, which, side],
            recv_sem=xr_sem.at[it, which, side],
            device_id={"row": sides[("row", side)][1]},
            device_id_type=pl.DeviceIdType.MESH,
        )

    def planes_of(side, n):
        first, end = (depth - radius, depth) if side == 0 else (0, radius)
        first, end = max(first, n * GROUP), min(end, (n + 1) * GROUP)
        return first, end - first

    pieces = (
        [[planes_of(side, n) + (0, CHUNK) for side in range(2)] for n in range(depth // GROUP)],
        [[(first, radius, r, 8) for first in (depth - radius, 0)] for r in range(0, CHUNK, 8)],
    )

    def slab_copy(buf, it, which, c, piece, side):
        first, count, r, rows = pieces[which][piece][side]
        moved = -depth if side == 0 else depth
        span = pl.ds(begin(c, r, 8), rows)
        return pltpu.make_async_remote_copy(
            src_ref=buf.at[it, pl.ds(radius + first, count), span, :],
            dst_ref=buf.at[it, pl.ds(radius + first + moved, count), span, :],
            send_sem=zs_sem.at[it, which, c, piece, side],
            recv_sem=zr_sem.at[it, which, c, piece, side],
            device_id={"slab": sides[("slab", side)][1]},
            device_id_type=pl.DeviceIdType.MESH,
        )

    def start(axis, side, make, also=True):
        @pl.when(sides[(axis, side)][0] & also)
        def _():
            make(side).start()

    def recv(axis, side, make, also=True):
        @pl.when(sides[(axis, 1 - side)][0] & also)
        def _():
            make(side).wait_recv()

    def sent(axis, side, make):
        @pl.when(sides[(axis, side)][0])
        def _():
            make(side).wait_send()

    sends = []

    def x_make(it, which):
        buffer = ext if which == 0 else dext
        return functools.partial(row_copy, (buffer.at[it], halo), buffer, it, which)

    def z_make(it, which, c, piece):
        return functools.partial(slab_copy, bz if which == 0 else rz, it, which, c, piece)

    def x_start(it, which, p):
        near = p == 0
        for v in range(2):
            side = 1 - v if near else v
            start("row", side, x_make(it, which), parity == v)
        if near:
            sends.extend(("row", side, x_make(it, which)) for side in range(2))

    def x_recv(it, which, p):
        near = p == 0
        for v in range(2):
            recv("row", v if near else 1 - v, x_make(it, which), parity == v)

    def z_start(it, which, c, piece):
        for side in range(2):
            start("slab", side, z_make(it, which, c, piece))
            sends.append(("slab", side, z_make(it, which, c, piece)))

    def z_recv(it, which, c, only=None):
        for piece in range(len(pieces[which])) if only is None else [only]:
            for side in range(2):
                recv("slab", side, z_make(it, which, c, piece))

    for fetch in fetches[1:]:
        fetch.wait()

    kk = 3 * halo
    rest = height - CHUNK
    rest_begin = pl.multiple_of((1 - parity) * CHUNK, CHUNK)
    rk = rest + 2 * halo
    mirror = (
        lax.broadcasted_iota(jnp.int32, (LANES, LANES), 0) + lax.broadcasted_iota(jnp.int32, (LANES, LANES), 1)
        == taps - 1
    ).astype(F32)
    for source, ahead in ((tx_ref, txf_ref), (ty_ref, tyf_ref)):
        ahead[...] = jnp.zeros(ahead.shape, F32)
        ahead[:, 0:taps] = source[...]

    def turn(ahead, back):
        back[...] = jnp.dot(ahead[...], mirror, precision=lax.Precision.HIGHEST, preferred_element_type=F32)
    turn(tyf_ref, tyr_ref)

    lane = lax.broadcasted_iota(jnp.int32, (1, LANES), 1)
    blocks = range(width // LANES)

    def column_band(line):
        gap = lax.broadcasted_iota(jnp.int32, (LANES, LANES), 0) - lane
        ring = pltpu.roll(jnp.broadcast_to(line, (LANES, LANES)), LANES - radius, 1, stride=1, stride_axis=0)
        main = jnp.where((gap <= radius) & (gap >= -radius), ring, 0.0)
        short = jnp.broadcast_to(line, (halo, LANES))
        after = pltpu.roll(short, LANES - radius, 1, stride=1, stride_axis=0)
        after = jnp.where(lane >= LANES - radius, after, 0.0)
        before = pltpu.roll(short, LANES - halo - radius, 1, stride=1, stride_axis=0)
        before = jnp.where(lane < radius, before, 0.0)
        return main, after, before

    def store_band(w, z, band):
        for start, part in zip((0, LANES, LANES + halo), band):
            high, low = split(part)
            w[z, start:start + part.shape[0], 0:LANES] = high
            w[z, start:start + part.shape[0], LANES:2 * LANES] = low

    def store_rows(a):
        high = a.astype(BF16).astype(F32)
        low = a - high
        zero = jnp.zeros(a.shape, F32)
        first = jnp.concatenate([high, zero], axis=1)
        second = jnp.concatenate([low, zero], axis=1)
        return (first + pltpu.roll(second, kk, 1) + pltpu.roll(first, 2 * kk, 1)).astype(BF16)

    def row_band(line):
        return pltpu.roll(jnp.broadcast_to(line, (CHUNK, LANES)), halo - radius, 1, stride=1, stride_axis=0)

    def build_forward(z, carry):
        at = pl.ds(band_ref[z], 1)
        store_band(wf, z, column_band(tyr_ref[at, :]))
        af[z] = store_rows(row_band(txf_ref[at, :]))
        return carry

    def build_adjoint(z, carry):
        at = pl.ds(band_ref[z], 1)
        band = column_band(tyf_ref[at, :])
        store_band(wa, z, band)
        tzv = jnp.zeros((1, LANES), F32)
        for k in range(taps):
            tzv = jnp.where(lane == k, tz_ref[k], tzv)
        plane = slab * depth + z + radius - lane
        inside = (plane >= 0) & (plane < slabs_n * depth)
        cz = jnp.sum(jnp.where(inside, tzv, 0.0), axis=1, keepdims=True)
        main, after, before = [jnp.sum(part, axis=0, keepdims=True) for part in band]
        for j in blocks:
            total = main
            if j > 0:
                total = total + before
            if j < blocks[-1]:
                total = total + after
            scale[z, :, j * LANES:(j + 1) * LANES] = 1.0 / (total * cz)
        base = row_band(txr_ref[at, :])
        for c in range(chunks):
            at_row = row * height + (c - 1) * CHUNK + lax.broadcasted_iota(jnp.int32, (CHUNK, LANES), 1)
            inside = (at_row >= 0) & (at_row < rows_n * height)
            aa[z, c] = store_rows(base / jnp.sum(jnp.where(inside, base, 0.0), axis=1, keepdims=True))
        long = pltpu.roll(
            jnp.broadcast_to(txr_ref[at, :], (rest, LANES)), halo - radius, 1, stride=1, stride_axis=0)
        at_row = row * height + rest_begin - halo + lane
        inside = (at_row >= 0) & (at_row < rows_n * height)
        long = long / jnp.sum(jnp.where(inside, long, 0.0), axis=1, keepdims=True)
        high = long.astype(BF16).astype(F32)
        zero = jnp.zeros(long.shape, F32)
        first = jnp.concatenate([high, zero], axis=1)
        second = jnp.concatenate([long - high, zero], axis=1)
        ar[z] = (first + pltpu.roll(second, rk, 1) + pltpu.roll(first, 2 * rk, 1)).astype(BF16)
        return carry

    def blur_rows(a, v):
        high, low = split(v)
        return jnp.dot(a[:, :3 * kk], jnp.concatenate([high, high, low], axis=0), preferred_element_type=F32)

    def blur_columns(v, w):
        n = v.shape[0]
        parts = [v[:, b * LANES:(b + 1) * LANES] for b in blocks]
        wide = []
        for b in blocks:
            outer = pltpu.roll(parts[b - 1], 2 * halo, 1) if b > 0 else 0.0
            outer = jnp.where(lane < halo, parts[b + 1] if b < blocks[-1] else 0.0, outer)
            wide.append(jnp.concatenate([parts[b], outer], axis=1))
        wide = jnp.concatenate(split(jnp.concatenate(wide, axis=0)), axis=0)
        both = jnp.dot(wide[:, :LANES + 2 * halo], w, preferred_element_type=F32)
        m = n * len(blocks)
        made = both[:m, :LANES] + both[m:, :LANES] + both[:m, LANES:]
        return jnp.concatenate([made[b * n:(b + 1) * n] for b in blocks], axis=1)

    def edge(it, which, p):
        if p in (0, chunks - 1):
            x_recv(it, which, p)

    def planes(make, put, group=GROUP, finish=None, part=None):
        def body(n, carry):
            made = [make(n * group + i) for i in range(group)]
            if finish is not None:
                made = [finish(n * group + i, v) for i, v in enumerate(made)]
            for i, v in enumerate(made):
                put(n * group + i, v)
            return carry
        if part is None:
            lax.fori_loop(0, depth // group, body, 0, unroll=PASSES)
        else:
            body(part, 0)

    def stage_xy(it, p):
        edge(it, 0, p)
        c = begin(p)

        def make(z):
            return blur_rows(af[z], ext[it, z, pl.ds(c, kk), :])

        def finish(z, v):
            return blur_columns(v, wf[z])

        def put(z, v):
            bz[it, radius + z, pl.ds(c, CHUNK), :] = v
        for part in range(len(pieces[0])):
            planes(make, put, GROUP, finish, part)
            z_start(it, 0, p, part)

    def blur_depth(buf, it, tile, lanes, flip):
        total = None
        for k in range(taps):
            weight = tz_ref[taps - 1 - k] if flip else tz_ref[k]
            term = weight * buf[it, k:k + depth, tile, lanes]
            total = term if total is None else total + term
        return total

    def tiles(p):
        for r in range(0, CHUNK, 8):
            for l in range(0, width, LANES):
                yield pl.ds(begin(p, r, 8), 8), pl.ds(begin(p, halo + r, 8), 8), slice(l, l + LANES)

    def stage_ratio(it, p):
        for n, (tile, inner, lanes) in enumerate(tiles(p)):
            blurred = blur_depth(bz, it, tile, lanes, False)
            rz[it, radius:radius + depth, tile, lanes] = ext[0, :, inner, lanes] / blurred
            if (n + 1) % len(blocks) == 0:
                z_start(it, 1, p, n // len(blocks))

    def stage_zy(it, p):
        for r in range(0, CHUNK, 8):
            z_recv(it, 1, p, r // 8)
            for l in range(0, width, LANES):
                lanes = slice(l, l + LANES)
                mid[:, r:r + 8, lanes] = blur_depth(rz, it, pl.ds(begin(p, r, 8), 8), lanes, True)
        rows = pl.ds(begin(p, halo), CHUNK)

        def put(z, v):
            dext[it, z, rows, :] = v
        planes(lambda z: blur_columns(mid[z], wa[z]) * scale[z], put, depth)
        if p in (0, chunks - 1):
            x_start(it, 1, p)

    def stage_x(it, p):
        edge(it, 1, p)
        c = begin(p)
        inner = pl.ds(begin(p, halo), CHUNK)

        def make(z):
            return ext[it, z, inner, :] * blur_rows(aa[z, chunk(p)], dext[it, z, pl.ds(c, kk), :])

        def put(z, v):
            if it == ITERS - 1:
                out_ref[z, pl.ds(c, CHUNK), :] = v
            else:
                ext[it + 1, z, inner, :] = v
        planes(make, put)
        if it < ITERS - 1 and p in (0, chunks - 1):
            x_start(it + 1, 0, p)

    def stage_rest():
        edge(ITERS - 1, 1, chunks - 1)

        def make(z):
            high, low = split(dext[ITERS - 1, z, pl.ds(rest_begin, rk), :])
            v = jnp.dot(ar[z][:, :3 * rk], jnp.concatenate([high, high, low], axis=0), preferred_element_type=F32)
            return ext[ITERS - 1, z, pl.ds(pl.multiple_of(rest_begin + halo, CHUNK), rest), :] * v

        def put(z, v):
            out_ref[z, pl.ds(rest_begin, rest), :] = v
        planes(make, put, 8)

    clear("row", ext, 0)
    lax.fori_loop(0, depth, build_forward, 0, unroll=4)
    pl.semaphore_wait(barrier, sum(there.astype(jnp.int32) for there, _ in sides.values()))
    fetches[0].wait()
    for p in (0, chunks - 1):
        x_start(0, 0, p)
    started = 0
    for it in range(ITERS):
        order = chunk_order(chunks, it)
        for p in order[started:]:
            stage_xy(it, p)
        if it == 0:
            turn(txf_ref, txr_ref)
            lax.fori_loop(0, depth, build_adjoint, 0)
            for buffer in (bz, rz):
                for i in range(ITERS):
                    clear("slab", buffer, i)
            for i in range(ITERS):
                clear("row", dext, i)
            for i in range(1, ITERS):
                clear("row", ext, i)
        for p in order:
            z_recv(it, 0, p)
            stage_ratio(it, p)
        ready = list(range(chunks - 2)) if it < ITERS - 1 else []
        for n, p in enumerate(order[:-1]):
            stage_zy(it, p)
            have = order[:n + 1]
            for q in [q for q in ready if all(o in have for o in (q - 1, q, q + 1) if 0 <= o < chunks)]:
                ready.remove(q)
                stage_x(it, q)
        if it < ITERS - 1:
            for p in range(chunks - 3):
                stage_xy(it + 1, p)
            stage_zy(it, order[-1])
            stage_x(it, chunks - 2)
            stage_xy(it + 1, chunks - 3)
            stage_x(it, chunks - 1)
            started = chunks - 2
        else:
            early = [p for p in range(chunks) if abs(p - order[-1]) > 1]
            for p in early:
                stage_x(it, p)
            stage_zy(it, order[-1])
            if early == [0] and 3 * rk <= 2 * LANES:
                stage_rest()
            else:
                for p in range(chunks):
                    if p not in early:
                        stage_x(it, p)

    for axis, side, make in sends:
        sent(axis, side, make)


def solution(mesh):
    rows_n, slabs_n = mesh.shape["row"], mesh.shape["slab"]

    def on_device(observed, band_index, taps_x, taps_y, taps_z):
        depth, height, width = observed.shape
        bands, taps = taps_x.shape
        radius = taps // 2

        vmem = pl.BlockSpec(memory_space=pltpu.VMEM)
        hbm = pl.BlockSpec(memory_space=pltpu.HBM)
        chunks = height // CHUNK
        return pl.pallas_call(
            functools.partial(kernel, rows_n, slabs_n, taps),
            out_shape=jax.ShapeDtypeStruct(observed.shape, F32),
            in_specs=[hbm] * 5,
            out_specs=vmem,
            scratch_shapes=[
                pltpu.SMEM((depth,), jnp.int32),
                pltpu.SMEM((taps,), F32),
                pltpu.VMEM((bands, taps), F32),
                pltpu.VMEM((bands, taps), F32),
                pltpu.SemaphoreType.DMA((5,)),
            ] + [pltpu.VMEM((bands, LANES), F32)] * 4 + [
                pltpu.VMEM((ITERS, depth, height + 2 * CHUNK, width), F32),
                pltpu.VMEM((ITERS, depth, height + 2 * CHUNK, width), F32),
                pltpu.VMEM((ITERS, depth + 2 * radius, height, width), F32),
                pltpu.VMEM((ITERS, depth + 2 * radius, height, width), F32),
                pltpu.VMEM((depth, LANES + 2 * CHUNK, 2 * LANES), BF16),
                pltpu.VMEM((depth, LANES + 2 * CHUNK, 2 * LANES), BF16),
                pltpu.VMEM((depth, 1, width), F32),
                pltpu.VMEM((depth, CHUNK, 2 * LANES), BF16),
                pltpu.VMEM((depth, chunks, CHUNK, 2 * LANES), BF16),
                pltpu.VMEM((depth, height - CHUNK, 2 * LANES), BF16),
                pltpu.VMEM((depth, CHUNK, width), F32),
                pltpu.SemaphoreType.DMA((ITERS, 2, chunks, max(depth // GROUP, CHUNK // 8), 2)),
                pltpu.SemaphoreType.DMA((ITERS, 2, chunks, max(depth // GROUP, CHUNK // 8), 2)),
                pltpu.SemaphoreType.DMA((ITERS, 2, 2)),
                pltpu.SemaphoreType.DMA((ITERS, 2, 2)),
            ],
            compiler_params=pltpu.CompilerParams(
                collective_id=0, has_side_effects=True, vmem_limit_bytes=48 * 1024 * 1024
            ),
        )(
            *[pltpu.with_memory_space_constraint(v, pltpu.HBM) for v in (band_index, taps_z, taps_x, taps_y, observed)]
        )

    in_specs = (P(("grp", "slab"), "row", None), P("slab"), P(), P(), P())
    return jax.shard_map(
        on_device, mesh=mesh, in_specs=in_specs, out_specs=P(("grp", "slab"), "row", None), check_vma=False
    )
```
